256 devices in a mesh: cohort: 32 (over z, y), feat: 8 (over x, core).
Axes of the slice: x: 4, y: 4, z: 8, core: 2. Of those that a mesh axis runs over, the one named last changes fastest.
Arguments:
- b_factors: float32 [128, 8192, 256], P('cohort', 'feat'), may hold values from -0.375 to 0.375
- a_factors: float32 [128, 256, 8192], P('cohort', None, 'feat'), may hold values from -0.0625 to 0.0625
- ranks: int32 [128], P('cohort'), may hold values from 8 to 256, as said below
- probes: float32 [8192, 256], P('feat'), may hold values from -6 to 6
Outputs:
- subspace: float32 [8192, 256], P('feat')
The draws below stay inside these ranges and needn't reach their ends.
Inputs may be any that keep to these rules, and one draw needn't show every extreme that they name: `ranks`: each client's rank is 8 times a power of two; some client has rank 256 and some client has rank 8.
All inputs are finite; a program needn't handle non-finite values.
Results may differ from the reference program's by a relative error of at most 0.00011.
Values sent between devices are 32-bit elements; how exact they have to be, the bound alone decides.
A program may use at most 64 MiB of HBM per device.

```python
import math
import jax
import jax.numpy as jnp
from jax import lax

D = 8192
P_SIZE = 256
RMAX = 256
CLI_DEV = 4
ITERS = 2
NS_STEPS = 5
CLIENTS = 128


def draw_ranks(key, part):
    levels = (RMAX // 8).bit_length()
    top_level = levels - 1
    tier_key = jax.random.fold_in(key, 11)
    level_key = jax.random.fold_in(key, 23)
    top_key = jax.random.fold_in(key, 37)
    low_key = jax.random.fold_in(key, 41)
    tiers = jax.random.randint(tier_key, (CLIENTS // CLI_DEV,), max(top_level - 2, 0), top_level + 1)
    spread_tiers = jnp.repeat(tiers, CLI_DEV, total_repeat_length=CLIENTS)
    lowest = jnp.maximum(spread_tiers - 2, 0)
    powers = jax.random.randint(level_key, (CLIENTS,), lowest, spread_tiers + 1)
    ranks = jnp.left_shift(jnp.full((CLIENTS,), 8, jnp.int32), powers.astype(jnp.int32))
    chosen = jax.random.randint(top_key, (), 0, CLIENTS)
    offset = jax.random.randint(low_key, (), 1, CLIENTS)
    smallest = (chosen + offset) % CLIENTS
    ranks = ranks.at[chosen].set(RMAX)
    ranks = ranks.at[smallest].set(8)
    return ranks.astype(jnp.int32)


def block_levels(key, extent, split, least, high):
    factor_of = 1.0
    for axis_at, blocks in split:
        draws = jax.random.uniform(jax.random.fold_in(jax.random.fold_in(key, 6), axis_at), (blocks,), jnp.float32, least / len(split), high / len(split))
        factor_of = factor_of * jnp.repeat(jnp.exp(draws), extent[axis_at] // blocks).reshape((-1,) + (1,) * (len(extent) - 1 - axis_at))
    return factor_of


def gaussian(key, dims, spread, reach, pieces=(), held_as=jnp.bfloat16):
    values = spread * jax.random.normal(key, dims, jnp.float32)
    if pieces:
        values = values * block_levels(key, dims, pieces, -0.22, 0.18)
    return jnp.clip(values, -reach, reach).astype(held_as)


def setup_inputs(seed: int = 0) -> dict:
    key_of = jax.random.split(jax.random.key(seed), 5)
    return {
        "b_factors": gaussian(key_of[0], (CLIENTS, D, RMAX), RMAX ** -0.5, 0.375, ((0, 32), (1, 8)), jnp.float32),
        "a_factors": gaussian(key_of[1], (CLIENTS, RMAX, D), D ** -0.5, 0.0625, ((0, 32), (2, 8)), jnp.float32),
        "ranks": draw_ranks(jax.random.fold_in(key_of[4], 71), 0),
        "probes": gaussian(key_of[3], (D, P_SIZE), 1.0, 6.0, ((0, 8),), jnp.float32),
    }


def live_table(ranks):
    slots = jnp.arange(RMAX, dtype=jnp.int32)
    return (slots[None, :] < ranks[:, None]).astype(jnp.float32)

def probe_panel(b_factors, a_factors, live, basis):

    def add_client(total, item):
        left, right, mask_row = item
        coef = jnp.dot(right, basis, precision=lax.Precision.HIGHEST, preferred_element_type=jnp.float32) * mask_row[:, None]
        return (total + jnp.dot(left, coef, precision=lax.Precision.HIGHEST, preferred_element_type=jnp.float32), None)
    total, unused = lax.scan(add_client, jnp.zeros((D, P_SIZE), jnp.float32), (b_factors, a_factors, live))
    return total

def orthonormal(panel):
    gram = jnp.dot(panel.T, panel, precision=lax.Precision.HIGHEST, preferred_element_type=jnp.float32)
    scale = lax.rsqrt(jnp.trace(gram))
    iterate = panel * scale
    for turn in range(NS_STEPS):
        inner = jnp.dot(iterate.T, iterate, precision=lax.Precision.HIGHEST, preferred_element_type=jnp.float32)
        iterate = 1.5 * iterate - 0.5 * jnp.dot(iterate, inner, precision=lax.Precision.HIGHEST, preferred_element_type=jnp.float32)
    return iterate

def reference(b_factors, a_factors, ranks, probes):
    live = live_table(ranks)
    basis = probes
    for turn in range(ITERS):
        basis = orthonormal(probe_panel(b_factors, a_factors, live, basis))
    return math.sqrt(D) * basis
```

```python
import math

import jax
import jax.numpy as jnp
from jax import lax
from jax.sharding import PartitionSpec as P

D = 8192
NS_STEPS = 5


def small(left, right):
    return jnp.dot(left, right, precision=lax.Precision.HIGHEST, preferred_element_type=jnp.float32)


def big(spec, left, right):
    return jnp.einsum(
        spec, left, right, precision=lax.Precision.HIGH, preferred_element_type=jnp.float32
    )


def newton(gram):
    eye = jnp.eye(gram.shape[0], dtype=jnp.float32)
    total = None
    for turn in range(NS_STEPS):
        step = 1.5 * eye - 0.5 * gram
        total = step if total is None else small(total, step)
        if turn + 1 < NS_STEPS:
            gram = small(small(gram, step), step)
    return total


def on_device(b_factors, a_factors, ranks, probes):
    slots = jnp.arange(b_factors.shape[2], dtype=jnp.int32)
    live = (slots[None, :] < ranks[:, None]).astype(jnp.float32)[:, :, None]
    coef = lax.psum(big("crd,dp->crp", a_factors, probes), "feat") * live
    first = lax.psum(big("cdr,crp->dp", b_factors, coef), "cohort")
    gram_one = lax.psum(big("dp,dq->pq", first, first), "feat")
    coef = lax.psum(big("crd,dp->crp", a_factors, first), "feat") * live
    scale_one = lax.rsqrt(jnp.trace(gram_one))
    coef = coef * scale_one
    second = lax.psum(big("cdr,crp->dp", b_factors, coef), "cohort")
    turn_one = newton(gram_one * (scale_one * scale_one))
    gram_two = lax.psum(big("dp,dq->pq", second, second), "feat")
    gram_two = small(small(turn_one, gram_two), turn_one)
    scale_two = lax.rsqrt(jnp.trace(gram_two))
    turn_two = newton(gram_two * (scale_two * scale_two))
    turn = small(turn_one, turn_two) * (scale_two * math.sqrt(D))
    return big("dp,pq->dq", second, turn)


def solution(mesh):
    in_specs = (P("cohort", "feat", None), P("cohort", None, "feat"), P("cohort"), P("feat", None))
    out_specs = P("feat", None)
    return jax.shard_map(
        on_device, mesh=mesh, in_specs=in_specs, out_specs=out_specs, check_vma=False
    )
```

```python
import functools
import math

import jax
import jax.numpy as jnp
from jax import lax
from jax.experimental import pallas as pl
from jax.experimental.pallas import tpu as pltpu
from jax.sharding import PartitionSpec as P

D = 8192
NS_STEPS = 5
NX, NY, NZ = 4, 4, 8
MESH = pl.DeviceIdType.MESH
BF = jnp.bfloat16
F32 = jnp.float32


def rows(ref, start, size):
    if not isinstance(start, int):
        start = pl.multiple_of(start, 8)
    return ref.at[pl.ds(start, size), :]


class Link:
    def __init__(self, send, recv):
        self.send, self.recv, self.count, self.sent = send, recv, 0, []

    def copy(self, src, dst, device):
        copy = pltpu.make_async_remote_copy(
            src_ref=src,
            dst_ref=dst,
            send_sem=self.send.at[self.count],
            recv_sem=self.recv.at[self.count],
            device_id=device,
            device_id_type=MESH,
        )
        copy.start()
        self.count += 1
        self.sent.append(copy)
        return copy

    def drain(self):
        for copy in self.sent:
            copy.wait_send()
        self.sent = []


def take(copies):
    for copy in copies:
        copy.wait_recv()


def reduce_ring(link, work, into, base, at, n, size, right, left, slots):
    half, reach = size // 2, n // 2

    def shard(ref, index, offset, extent):
        return rows(ref, base + lax.rem(index + n, n) * size + offset, extent)

    def slot(way, step, offset, extent):
        return rows(slots, (way * reach + step) * size + offset, extent)

    ways = ((1, 0, right), (-1, half, left))
    coming = []
    for way, (sign, offset, device) in enumerate(ways):
        coming.append(
            [link.copy(shard(work, at + reach, offset, half), slot(way, 0, offset, half), device)]
        )
    ahead = []
    for way, (sign, offset, device) in enumerate(ways):
        ahead.append(
            link.copy(
                shard(work, at + sign * (reach - 1), half - offset, half),
                slot(way, 1, half - offset, half),
                device,
            )
        )
    for step in range(1, reach):
        yield
        for way, (sign, offset, device) in enumerate(ways):
            take(coming[way])
            skip, extent = (offset, half) if step == 1 else (0, size)
            target = shard(work, at + sign * (reach - step), skip, extent)
            target[...] = target[...] + slot(way, step - 1, skip, extent)[...]
            coming[way] = [link.copy(target, slot(way, step, skip, extent), device)]
            if step == 1:
                coming[way].append(ahead[way])
    yield
    take(coming[0])
    take(coming[1])
    shard(into, at, 0, size)[...] = (
        shard(work, at, 0, size)[...]
        + slot(0, reach - 1, 0, size)[...]
        + slot(1, reach - 1, 0, size)[...]
    )


def gather_ring(link, into, base, at, n, size, right, left, also=None):
    half, reach = size // 2, n // 2

    def shard(index, offset, extent):
        return rows(into, base + lax.rem(index + n, n) * size + offset, extent)

    def push(index, pieces, device):
        return [
            link.copy(shard(index, offset, extent), shard(index, offset, extent), device)
            for offset, extent in pieces
        ]

    ways = ((1, 0, right), (-1, half, left))
    whole, split = lambda offset: ((0, size),), lambda offset: ((offset, half), (half - offset, half))
    coming, late = [], []
    for sign, offset, device in ways:
        coming.append(push(at, (split if reach == 2 else whole)(offset), device))
    if also is not None:
        also(shard(at, 0, size))
    for step in range(1, reach):
        yield
        for way, (sign, offset, device) in enumerate(ways):
            origin = at - sign * step
            if step == reach - 1:
                take(coming[way][:1])
                late.append((origin, coming[way][1:], half - offset))
                if also is not None:
                    also(shard(origin, offset, half))
                coming[way] = push(origin, ((offset, half),), device)
            else:
                take(coming[way])
                pieces = split if step == reach - 2 else whole
                if also is not None:
                    also(shard(origin, 0, size))
                coming[way] = push(origin, pieces(offset), device)
    yield
    for origin, copies, offset in late:
        take(copies)
        if also is not None:
            also(shard(origin, offset, half))
    for way, (sign, offset, device) in enumerate(ways):
        take(coming[way])
        if also is not None:
            also(shard(at - sign * reach, offset, half))


def feat_total(link, place, work, into, near, slots, extent):
    half = extent // 2
    quarter = half // NX
    mine, other = place["core"] * half, (1 - place["core"]) * half
    pairs = []
    for offset in (2, 1, 3, 0):
        start = lax.rem(place["x"] + offset, NX) * quarter
        pairs.append(
            (
                start,
                link.copy(
                    rows(work, other + start, quarter), rows(near, start, quarter), place["partner"]
                ),
            )
        )
    yield
    for start, copy in pairs:
        copy.wait_recv()
        target = rows(work, mine + start, quarter)
        target[...] = target[...] + rows(near, start, quarter)[...]
    right, left = place["right_x"], place["left_x"]
    yield from reduce_ring(
        link, work, into, mine, place["x"], NX, quarter, right, left, slots
    )
    shared = []

    def also(ref):
        shared.append(link.copy(ref, ref, place["partner"]))

    yield from gather_ring(link, into, mine, place["x"], NX, quarter, right, left, also)
    yield
    take(shared)


def cohort_total(link, place, work, into, slots, base, extent, order):
    first, second = order
    n, m = place["size_" + first], place["size_" + second]
    size, small = extent // n, extent // n // m
    i, j = place[first], place[second]
    cut = n * size
    ring = (place["right_" + first], place["left_" + first])
    inner = (place["right_" + second], place["left_" + second])
    near = base + i * size
    yield from reduce_ring(link, work, work, base, i, n, size, *ring, rows(slots, 0, cut))
    yield from reduce_ring(
        link, work, into, near, j, m, small, *inner, rows(slots, cut, m * small)
    )
    yield from gather_ring(link, into, near, j, m, small, *inner)
    yield from gather_ring(link, into, base, i, n, size, *ring)


def run(*streams):
    streams = list(streams)
    while streams:
        for stream in list(streams):
            try:
                next(stream)
            except StopIteration:
                streams.remove(stream)


def halves(value):
    high = value.astype(BF)
    return high, (value - high.astype(F32)).astype(BF)


def dot(left, right, dims=(((1,), (0,)), ((), ()))):
    return lax.dot_general(left, right, dims, preferred_element_type=F32)


def product(left, right, dims=(((1,), (0,)), ((), ()))):
    (lh, ll), (rh, rl) = left, right
    return dot(lh, rh, dims) + (dot(lh, rl, dims) + dot(ll, rh, dims))


def times(left, right):
    return product(halves(left), halves(right))


def inverse_root(total):
    guess = lax.rsqrt(total)
    return guess * (1.5 - 0.5 * total * guess * guess)


def diagonal(p):
    return lax.broadcasted_iota(jnp.int32, (p, p), 0) == lax.broadcasted_iota(jnp.int32, (p, p), 1)


def root_of_trace(gram):
    total = jnp.sum(jnp.where(diagonal(gram.shape[0]), gram, 0.0), keepdims=True)
    return inverse_root(total)


def newton(gram, step, turn):
    p = gram.shape[0]
    for at in range(NS_STEPS):
        step[...] = jnp.where(diagonal(p), 1.5, 0.0) - 0.5 * gram[...]
        if at == 0:
            turn[...] = step[...]
        else:
            turn[...] = times(turn[...], step[...])
        if at + 1 < NS_STEPS:
            yield
            gram[...] = times(gram[...], step[...])
            yield
            gram[...] = times(gram[...], step[...])
            yield


def kernel(
    ranks, b_hbm, a_hbm, p_hbm, out,
    stage, a_high, a_low, b_high, b_low, y_high, y_low, c_high, c_low,
    work_a, into_a, near_a, slots_a,
    work_b, into_b, near_b, slots_b,
    work_g, into_g, near_g, slots_g,
    panel_one, panel_two, whole_one, whole_two, rings_one, rings_two,
    probe, gram, step, turn_one, turn_two,
    send, recv, local,
):
    clients, features, rank = b_hbm.shape
    p = probe.shape[1]
    slots = clients * rank
    cohort, feat = lax.axis_index("cohort"), lax.axis_index("feat")
    z, y = lax.div(cohort, NY), lax.rem(cohort, NY)
    x, core = lax.div(feat, 2), lax.rem(feat, 2)
    place = {
        "x": x, "y": y, "z": z, "core": core, "size_y": NY, "size_z": NZ,
        "partner": (cohort, x * 2 + 1 - core),
        "right_x": (cohort, lax.rem(x + 1, NX) * 2 + core),
        "left_x": (cohort, lax.rem(x + NX - 1, NX) * 2 + core),
        "right_y": (z * NY + lax.rem(y + 1, NY), feat),
        "left_y": (z * NY + lax.rem(y + NY - 1, NY), feat),
        "right_z": (lax.rem(z + 1, NZ) * NY + y, feat),
        "left_z": (lax.rem(z + NZ - 1, NZ) * NY + y, feat),
    }
    peers = [place[k] for k in ("partner", "right_x", "left_x", "right_y", "left_y", "right_z", "left_z")]

    load_p = pltpu.make_async_copy(p_hbm, probe, local.at[0])
    load_p.start()
    load_a = [
        pltpu.make_async_copy(a_hbm.at[c], stage.at[pl.ds(c * rank, rank), :], local.at[1 + c])
        for c in range(clients)
    ]
    for copy in load_a:
        copy.start()

    barrier = pltpu.get_barrier_semaphore()
    for peer in peers:
        pl.semaphore_signal(barrier, inc=1, device_id=peer, device_id_type=MESH)

    link = Link(send, recv)
    load_p.wait()
    y_high[...], y_low[...] = halves(probe[...])
    for c in range(clients):
        load_a[c].wait()
        at = pl.ds(c * rank, rank)
        a_high[at, :], a_low[at, :] = halves(stage[at, :])
    pl.semaphore_wait(barrier, len(peers))

    def client_coef(c):
        at = pl.ds(pl.multiple_of(c * rank, 8), rank)
        total = product((a_high[at, :], a_low[at, :]), (y_high[...], y_low[...]))
        live = lax.broadcasted_iota(jnp.int32, total.shape, 0) < ranks[c]
        return jnp.where(live, total, 0.0)

    def coef_half(work, which, half):
        def one(k, carry):
            start = which * half + k * rank
            work[pl.ds(pl.multiple_of(start, 8), rank), :] = client_coef(which * (clients // 2) + k)
            return carry
        lax.fori_loop(0, clients // 2, one, 0)

    coef_half(work_a, 1 - core, slots // 2)
    total = feat_total(link, place, work_a, into_a, near_a, slots_a, slots)
    next(total)
    coef_half(work_a, core, slots // 2)

    def b_stream():
        def fetch(c):
            return pltpu.make_async_copy(
                b_hbm.at[c], stage.at[:, pl.ds(c * rank, rank)], local.at[1 + clients + c]
            )
        loads = [fetch(c) for c in range(clients)]
        for copy in loads:
            copy.start()
        for c in range(clients):
            loads[c].wait()
            across = pl.ds(c * rank, rank)
            for k in range(2):
                at = pl.ds(k * (features // 2), features // 2)
                b_high[at, across], b_low[at, across] = halves(stage[at, across])
                yield

    run(total, b_stream())

    def panel_half(work, which):
        at = pl.ds(which * (features // 2), features // 2)
        work[at, :] = product((b_high[at, :], b_low[at, :]), (c_high[...], c_low[...]))

    def panel_total(work, into, rings, *others):
        half = features // 2
        panel_half(work, 0)
        upper = cohort_total(link, place, work, into, rows(rings, 0, 2 * half), 0, half, ("y", "z"))
        next(upper)
        panel_half(work, 1)
        lower = cohort_total(
            link, place, work, into, rows(rings, 2 * half, 2 * half), half, half, ("z", "y")
        )
        run(upper, lower, *others)

    c_high[...], c_low[...] = halves(into_a[...])
    panel_total(panel_one, whole_one, rings_one)
    link.drain()

    contract_rows = (((0,), (0,)), ((), ()))
    half_c, half_g = slots // 2, p // 2
    half = half_c + half_g
    y_high[...], y_low[...] = halves(whole_one[...])
    local_gram = product((y_high[...], y_low[...]), (y_high[...], y_low[...]), contract_rows)
    for which in range(2):
        work_b[pl.ds(which * half + half_c, half_g), :] = local_gram[which * half_g:(which + 1) * half_g]
    coef_half(work_b, 1 - core, half)
    total = feat_total(link, place, work_b, into_b, near_b, slots_b, slots + p)
    next(total)
    coef_half(work_b, core, half)
    run(total)

    for which in range(2):
        gram[pl.ds(which * half_g, half_g), :] = into_b[pl.ds(which * half + half_c, half_g), :]
    scale = root_of_trace(gram[...])
    gram[...] = gram[...] * (scale * scale)
    for which in range(2):
        at = pl.ds(which * half_c, half_c)
        c_high[at, :], c_low[at, :] = halves(into_b[pl.ds(which * half, half_c), :] * scale)
    panel_total(panel_two, whole_two, rings_two, newton(gram, step, turn_one))

    y_high[...], y_low[...] = halves(whole_two[...])
    work_g[...] = product((y_high[...], y_low[...]), (y_high[...], y_low[...]), contract_rows)
    run(feat_total(link, place, work_g, into_g, near_g, slots_g, p))
    gram[...] = times(times(turn_one[...], into_g[...]), turn_one[...])
    scale = root_of_trace(gram[...])
    gram[...] = gram[...] * (scale * scale)
    run(newton(gram, step, turn_two))
    last = times(turn_one[...], turn_two[...]) * (scale * math.sqrt(D))
    out[...] = product((y_high[...], y_low[...]), halves(last))
    link.drain()


def on_device(b_factors, a_factors, ranks, probes):
    clients, features, rank = b_factors.shape
    p = probes.shape[1]
    slots = clients * rank
    vm = pltpu.VMEM

    def feat_space(extent):
        return [
            vm((extent, p), F32), vm((extent, p), F32), vm((extent // 2, p), F32),
            vm((extent // 2, p), F32),
        ]

    scratch = (
        [vm((slots, features), F32)]
        + [vm((slots, features), BF)] * 2
        + [vm((features, slots), BF)] * 2
        + [vm((features, p), BF)] * 2
        + [vm((slots, p), BF)] * 2
        + feat_space(slots) + feat_space(slots + p) + feat_space(p)
        + [vm((features, p), F32)] * 4
        + [vm((2 * features, p), F32)] * 2
        + [vm((features, p), F32)]
        + [vm((p, p), F32)] * 4
        + [pltpu.SemaphoreType.DMA((200,)), pltpu.SemaphoreType.DMA((200,)), pltpu.SemaphoreType.DMA((1 + 2 * clients,))]
    )
    anywhere = pl.BlockSpec(memory_space=pl.ANY)
    return pl.pallas_call(
        kernel,
        out_shape=jax.ShapeDtypeStruct((features, p), F32),
        in_specs=[pl.BlockSpec(memory_space=pltpu.SMEM), anywhere, anywhere, anywhere],
        out_specs=pl.BlockSpec(memory_space=pltpu.VMEM),
        scratch_shapes=scratch,
        compiler_params=pltpu.CompilerParams(
            collective_id=0, has_side_effects=True, vmem_limit_bytes=60 << 20
        ),
    )(ranks, b_factors, a_factors, probes)


def solution(mesh):
    in_specs = (P("cohort", "feat", None), P("cohort", None, "feat"), P("cohort"), P("feat", None))
    out_specs = P("feat", None)
    return jax.shard_map(
        on_device, mesh=mesh, in_specs=in_specs, out_specs=out_specs, check_vma=False
    )
```

```python
import functools
import math

import jax
import jax.numpy as jnp
from jax import lax
from jax.experimental import pallas as pl
from jax.experimental.pallas import tpu as pltpu
from jax.sharding import PartitionSpec as P

D = 8192
NS_STEPS = 5
NX, NY, NZ = 4, 4, 8
MESH = pl.DeviceIdType.MESH
FAR_FIRST = {4: (2, 1, 3), 8: (4, 3, 5, 2, 6, 1, 7)}
BF = jnp.bfloat16
F32 = jnp.float32


def rows(ref, start, size):
    if not isinstance(start, int):
        start = pl.multiple_of(start, 8)
    return ref.at[pl.ds(start, size), :]


class Link:
    def __init__(self, send, recv):
        self.send, self.recv, self.count, self.sent = send, recv, 0, []

    def copy(self, src, dst, device):
        copy = pltpu.make_async_remote_copy(
            src_ref=src,
            dst_ref=dst,
            send_sem=self.send.at[self.count],
            recv_sem=self.recv.at[self.count],
            device_id=device,
            device_id_type=MESH,
        )
        copy.start()
        self.count += 1
        self.sent.append(copy)
        return copy

    def drain(self):
        for copy in self.sent:
            copy.wait_send()
        self.sent = []


def take(copies):
    for copy in copies:
        copy.wait_recv()


def reduce_direct(link, work, into, base, at, n, size, device, slots, ready=None):
    coming = []
    for offset in FAR_FIRST[n]:
        start = base + lax.rem(at + offset, n) * size
        if ready is not None:
            ready(offset)
        coming.append(
            link.copy(
                rows(work, start, size), rows(slots, (offset - 1) * size, size), device(offset)
            )
        )
    if ready is not None:
        ready(0)
    yield
    take(coming)
    total = rows(work, base + at * size, size)[...]
    for step in range(n - 1):
        total = total + rows(slots, step * size, size)[...]
    rows(into, base + at * size, size)[...] = total


def gather_direct(link, into, base, at, n, size, device, also=None):
    own = rows(into, base + at * size, size)
    coming = [(offset, link.copy(own, own, device(offset))) for offset in FAR_FIRST[n]]
    if also is not None:
        also(own)
    yield
    for offset, copy in reversed(coming):
        copy.wait_recv()
        if also is not None:
            also(rows(into, base + lax.rem(at + n - offset, n) * size, size))


def reduce_pair_steps(link, work, into, base, at, n, size, device, slots):
    half = size // 2

    def shard(offset, skip, extent):
        return rows(work, base + lax.rem(at + offset + n, n) * size + skip, extent)

    def slot(index, extent):
        return rows(slots, index * size, extent)

    signs = ((1, 0, 0), (-1, half, 4))
    coming, straight, joined = {}, [], []
    for sign, skip, first in signs:
        coming[sign] = [
            link.copy(shard(4, skip, half), slot(first, half), device(2 * sign)),
            link.copy(shard(3 * sign, 0, size), slot(first + 1, size), device(sign)),
        ]
    for sign, skip, first in signs:
        straight.append(link.copy(shard(sign, 0, size), slot(first + 2, size), device(sign)))
    yield
    for sign, skip, first in signs:
        take(coming[sign])
        target = shard(2 * sign, 0, size)
        target[...] = target[...] + slot(first + 1, size)[...]
        part = shard(2 * sign, skip, half)
        part[...] = part[...] + slot(first, half)[...]
        joined.append(link.copy(target, slot(first + 3, size), device(2 * sign)))
    yield
    take(straight)
    take(joined)
    total = shard(0, 0, size)[...]
    for index in (2, 3, 6, 7):
        total = total + slot(index, size)[...]
    rows(into, base + at * size, size)[...] = total


def gather_pair_steps(link, into, base, at, n, size, device):
    half = size // 2

    def shard(offset, skip=0, extent=size):
        return rows(into, base + lax.rem(at + offset + n, n) * size + skip, extent)

    signs = ((1, 0), (-1, half))
    far = {sign: link.copy(shard(0), shard(0), device(2 * sign)) for sign, skip in signs}
    near = [link.copy(shard(0), shard(0), device(sign)) for sign, skip in signs]
    yield
    last = []
    for sign, skip in signs:
        far[sign].wait_recv()
        passed = shard(-2 * sign, skip, half)
        last.append(link.copy(passed, passed, device(2 * sign)))
        passed = shard(-2 * sign)
        last.append(link.copy(passed, passed, device(sign)))
    yield
    take(near)
    take(last)


def feat_total(link, place, work, into, near, slots, extent):
    half = extent // 2
    quarter = half // NX
    x, mine, other = place["x"], place["core"] * half, (1 - place["core"]) * half
    pairs = {}
    for offset in FAR_FIRST[NX] + (0,):
        start = lax.rem(x + offset, NX) * quarter
        pairs[offset] = (
            start,
            link.copy(rows(work, other + start, quarter), rows(near, start, quarter), place["partner"]),
        )
    yield

    def ready(offset):
        start, copy = pairs[offset]
        copy.wait_recv()
        target = rows(work, mine + start, quarter)
        target[...] = target[...] + rows(near, start, quarter)[...]

    yield from reduce_direct(
        link, work, into, mine, x, NX, quarter, place["along_x"], slots, ready
    )
    shared = []

    def also(ref):
        shared.append(link.copy(ref, ref, place["partner"]))

    yield from gather_direct(link, into, mine, x, NX, quarter, place["along_x"], also)
    yield
    take(shared)


def upper_total(link, place, work, into, slots, base, extent):
    y, z = place["y"], place["z"]
    size, small = extent // NY, extent // NY // NZ
    near = base + y * size
    along_y, along_z = place["along_y"], place["along_z"]
    yield from reduce_direct(link, work, work, base, y, NY, size, along_y, rows(slots, 0, extent))
    yield from reduce_direct(link, work, into, near, z, NZ, small, along_z, rows(slots, extent, size))
    yield from gather_direct(link, into, near, z, NZ, small, along_z)
    yield from gather_direct(link, into, base, y, NY, size, along_y)


def lower_total(link, place, work, into, slots, base, extent):
    y, z = place["y"], place["z"]
    size, small = extent // NZ, extent // NZ // NY
    near = base + z * size
    along_y, along_z = place["along_y"], place["along_z"]
    yield from reduce_pair_steps(link, work, work, base, z, NZ, size, along_z, rows(slots, 0, extent))
    yield from reduce_direct(link, work, into, near, y, NY, small, along_y, rows(slots, extent, size))
    yield from gather_direct(link, into, near, y, NY, small, along_y)
    yield from gather_pair_steps(link, into, base, z, NZ, size, along_z)


def run(*streams):
    streams = list(streams)
    while streams:
        for stream in list(streams):
            try:
                next(stream)
            except StopIteration:
                streams.remove(stream)


def halves(value):
    high = value.astype(BF)
    return high, (value - high.astype(F32)).astype(BF)


def dot(left, right, dims=(((1,), (0,)), ((), ()))):
    return lax.dot_general(left, right, dims, preferred_element_type=F32)


def product(left, right, dims=(((1,), (0,)), ((), ()))):
    (lh, ll), (rh, rl) = left, right
    return dot(lh, rh, dims) + (dot(lh, rl, dims) + dot(ll, rh, dims))


def times(left, right):
    return product(halves(left), halves(right))


def inverse_root(total):
    guess = lax.rsqrt(total)
    return guess * (1.5 - 0.5 * total * guess * guess)


def diagonal(p):
    return lax.broadcasted_iota(jnp.int32, (p, p), 0) == lax.broadcasted_iota(jnp.int32, (p, p), 1)


def root_of_trace(gram):
    total = jnp.sum(jnp.where(diagonal(gram.shape[0]), gram, 0.0), keepdims=True)
    return inverse_root(total)


def newton(gram, step, turn):
    p = gram.shape[0]
    for at in range(NS_STEPS):
        step[...] = jnp.where(diagonal(p), 1.5, 0.0) - 0.5 * gram[...]
        if at == 0:
            turn[...] = step[...]
        else:
            turn[...] = times(turn[...], step[...])
        if at + 1 < NS_STEPS:
            yield
            gram[...] = times(gram[...], step[...])
            yield
            gram[...] = times(gram[...], step[...])
            yield


def kernel(
    ranks, b_hbm, a_hbm, p_hbm, out,
    stage, a_high, a_low, b_high, b_low, y_high, y_low, c_high, c_low,
    work_a, into_a, near_a, slots_a,
    work_b, into_b, near_b, slots_b,
    work_g, into_g, near_g, slots_g,
    panel_one, panel_two, whole_one, whole_two, rings_one, rings_two,
    probe, gram, step, turn_one, turn_two,
    send, recv, local,
):
    clients, features, rank = b_hbm.shape
    p = probe.shape[1]
    slots = clients * rank
    cohort, feat = lax.axis_index("cohort"), lax.axis_index("feat")
    z, y = lax.div(cohort, NY), lax.rem(cohort, NY)
    x, core = lax.div(feat, 2), lax.rem(feat, 2)
    place = {
        "x": x, "y": y, "z": z, "core": core,
        "partner": (cohort, x * 2 + 1 - core),
        "along_x": lambda d: (cohort, lax.rem(x + d + NX, NX) * 2 + core),
        "along_y": lambda d: (z * NY + lax.rem(y + d + NY, NY), feat),
        "along_z": lambda d: (lax.rem(z + d + NZ, NZ) * NY + y, feat),
    }
    peers = [place["partner"]]
    for axis, n in (("along_x", NX), ("along_y", NY), ("along_z", NZ)):
        peers += [place[axis](d) for d in range(1, n)]

    load_p = pltpu.make_async_copy(p_hbm, probe, local.at[0])
    load_p.start()
    load_a = [
        pltpu.make_async_copy(a_hbm.at[c], stage.at[pl.ds(c * rank, rank), :], local.at[1 + c])
        for c in range(clients)
    ]
    for copy in load_a:
        copy.start()

    barrier = pltpu.get_barrier_semaphore()
    for peer in peers:
        pl.semaphore_signal(barrier, inc=1, device_id=peer, device_id_type=MESH)

    link = Link(send, recv)
    load_p.wait()
    y_high[...], y_low[...] = halves(probe[...])
    for c in range(clients):
        load_a[c].wait()
        at = pl.ds(c * rank, rank)
        a_high[at, :], a_low[at, :] = halves(stage[at, :])
    pl.semaphore_wait(barrier, len(peers))

    def client_coef(c):
        at = pl.ds(pl.multiple_of(c * rank, 8), rank)
        total = product((a_high[at, :], a_low[at, :]), (y_high[...], y_low[...]))
        live = lax.broadcasted_iota(jnp.int32, total.shape, 0) < ranks[c]
        return jnp.where(live, total, 0.0)

    def coef_half(work, which, half):
        def one(k, carry):
            start = which * half + k * rank
            work[pl.ds(pl.multiple_of(start, 8), rank), :] = client_coef(which * (clients // 2) + k)
            return carry
        lax.fori_loop(0, clients // 2, one, 0)

    coef_half(work_a, 1 - core, slots // 2)
    total = feat_total(link, place, work_a, into_a, near_a, slots_a, slots)
    next(total)
    coef_half(work_a, core, slots // 2)

    def b_stream():
        def fetch(c):
            return pltpu.make_async_copy(
                b_hbm.at[c], stage.at[:, pl.ds(c * rank, rank)], local.at[1 + clients + c]
            )
        loads = [fetch(c) for c in range(clients)]
        for copy in loads:
            copy.start()
        for c in range(clients):
            loads[c].wait()
            across = pl.ds(c * rank, rank)
            for k in range(2):
                at = pl.ds(k * (features // 2), features // 2)
                b_high[at, across], b_low[at, across] = halves(stage[at, across])
                yield

    run(total, b_stream())

    def panel_half(work, which):
        at = pl.ds(which * (features // 2), features // 2)
        work[at, :] = product((b_high[at, :], b_low[at, :]), (c_high[...], c_low[...]))

    def panel_total(work, into, rings, *others):
        half = features // 2
        panel_half(work, 1)
        lower = lower_total(link, place, work, into, rows(rings, 2 * half, 2 * half), half, half)
        next(lower)
        panel_half(work, 0)
        upper = upper_total(link, place, work, into, rows(rings, 0, 2 * half), 0, half)
        next(upper)
        for stream in (lower, upper, lower, upper, lower, lower, upper, lower, upper, lower):
            for other in others:
                next(other, None)
                next(other, None)
            next(stream, None)
        for other in others:
            run(other)

    c_high[...], c_low[...] = halves(into_a[...])
    panel_total(panel_one, whole_one, rings_one)
    link.drain()

    contract_rows = (((0,), (0,)), ((), ()))
    half_c, half_g = slots // 2, p // 2
    half = half_c + half_g
    y_high[...], y_low[...] = halves(whole_one[...])
    local_gram = product((y_high[...], y_low[...]), (y_high[...], y_low[...]), contract_rows)
    for which in range(2):
        work_b[pl.ds(which * half + half_c, half_g), :] = local_gram[which * half_g:(which + 1) * half_g]
    coef_half(work_b, 1 - core, half)
    total = feat_total(link, place, work_b, into_b, near_b, slots_b, slots + p)
    next(total)
    coef_half(work_b, core, half)
    run(total)

    for which in range(2):
        gram[pl.ds(which * half_g, half_g), :] = into_b[pl.ds(which * half + half_c, half_g), :]
    scale = root_of_trace(gram[...])
    gram[...] = gram[...] * (scale * scale)
    for which in range(2):
        at = pl.ds(which * half_c, half_c)
        c_high[at, :], c_low[at, :] = halves(into_b[pl.ds(which * half, half_c), :] * scale)
    panel_total(panel_two, whole_two, rings_two, newton(gram, step, turn_one))

    y_high[...], y_low[...] = halves(whole_two[...])
    work_g[...] = product((y_high[...], y_low[...]), (y_high[...], y_low[...]), contract_rows)
    run(feat_total(link, place, work_g, into_g, near_g, slots_g, p))
    gram[...] = times(times(turn_one[...], into_g[...]), turn_one[...])
    scale = root_of_trace(gram[...])
    gram[...] = gram[...] * (scale * scale)
    run(newton(gram, step, turn_two))
    last = times(turn_one[...], turn_two[...]) * (scale * math.sqrt(D))
    out[...] = product((y_high[...], y_low[...]), halves(last))
    link.drain()


def on_device(b_factors, a_factors, ranks, probes):
    clients, features, rank = b_factors.shape
    p = probes.shape[1]
    slots = clients * rank
    vm = pltpu.VMEM

    def feat_space(extent):
        return [
            vm((extent, p), F32), vm((extent, p), F32), vm((extent // 2, p), F32),
            vm((extent // 2, p), F32),
        ]

    scratch = (
        [vm((slots, features), F32)]
        + [vm((slots, features), BF)] * 2
        + [vm((features, slots), BF)] * 2
        + [vm((features, p), BF)] * 2
        + [vm((slots, p), BF)] * 2
        + feat_space(slots) + feat_space(slots + p) + feat_space(p)
        + [vm((features, p), F32)] * 4
        + [vm((2 * features, p), F32)] * 2
        + [vm((features, p), F32)]
        + [vm((p, p), F32)] * 4
        + [pltpu.SemaphoreType.DMA((200,)), pltpu.SemaphoreType.DMA((200,)), pltpu.SemaphoreType.DMA((1 + 2 * clients,))]
    )
    anywhere = pl.BlockSpec(memory_space=pl.ANY)
    return pl.pallas_call(
        kernel,
        out_shape=jax.ShapeDtypeStruct((features, p), F32),
        in_specs=[pl.BlockSpec(memory_space=pltpu.SMEM), anywhere, anywhere, anywhere],
        out_specs=pl.BlockSpec(memory_space=pltpu.VMEM),
        scratch_shapes=scratch,
        compiler_params=pltpu.CompilerParams(
            collective_id=0, has_side_effects=True, vmem_limit_bytes=60 << 20
        ),
    )(ranks, b_factors, a_factors, probes)


def solution(mesh):
    in_specs = (P("cohort", "feat", None), P("cohort", None, "feat"), P("cohort"), P("feat", None))
    out_specs = P("feat", None)
    return jax.shard_map(
        on_device, mesh=mesh, in_specs=in_specs, out_specs=out_specs, check_vma=False
    )
```

```python
import functools
import math

import jax
import jax.numpy as jnp
from jax import lax
from jax.experimental import pallas as pl
from jax.experimental.pallas import tpu as pltpu
from jax.sharding import PartitionSpec as P

D = 8192
NS_STEPS = 5
NX, NY, NZ = 4, 4, 8
MESH = pl.DeviceIdType.MESH
FAR_FIRST = {4: (2, 1, 3), 8: (4, 3, 5, 2, 6, 1, 7)}
BF = jnp.bfloat16
F32 = jnp.float32


def rows(ref, start, size):
    if not isinstance(start, int):
        start = pl.multiple_of(start, 8)
    return ref.at[pl.ds(start, size), :]


class Link:
    def __init__(self, send, recv):
        self.send, self.recv, self.count, self.sent = send, recv, 0, []

    def copy(self, src, dst, device):
        copy = pltpu.make_async_remote_copy(
            src_ref=src,
            dst_ref=dst,
            send_sem=self.send.at[self.count],
            recv_sem=self.recv.at[self.count],
            device_id=device,
            device_id_type=MESH,
        )
        copy.start()
        self.count += 1
        self.sent.append(copy)
        return copy

    def drain(self):
        for copy in self.sent:
            copy.wait_send()
        self.sent = []


def take(copies):
    for copy in copies:
        copy.wait_recv()


def reduce_direct(link, work, into, base, at, n, size, device, slots, ready=None):
    coming = []
    for offset in FAR_FIRST[n]:
        start = base + lax.rem(at + offset, n) * size
        if ready is not None:
            ready(offset)
        coming.append(
            link.copy(
                rows(work, start, size), rows(slots, (offset - 1) * size, size), device(offset)
            )
        )
    if ready is not None:
        ready(0)
    yield
    take(coming)
    total = rows(work, base + at * size, size)[...]
    for step in range(n - 1):
        total = total + rows(slots, step * size, size)[...]
    rows(into, base + at * size, size)[...] = total


def gather_direct(link, into, base, at, n, size, device, also=None):
    own = rows(into, base + at * size, size)
    coming = [(offset, link.copy(own, own, device(offset))) for offset in FAR_FIRST[n]]
    if also is not None:
        also(own)
    yield
    for offset, copy in reversed(coming):
        copy.wait_recv()
        if also is not None:
            also(rows(into, base + lax.rem(at + n - offset, n) * size, size))


def reduce_pair_steps(link, work, into, base, at, n, size, device, slots):
    half = size // 2

    def shard(offset, skip, extent):
        return rows(work, base + lax.rem(at + offset + n, n) * size + skip, extent)

    def slot(index, extent):
        return rows(slots, index * size, extent)

    signs = ((1, 0, 0), (-1, half, 4))
    coming, straight, joined = {}, [], []
    for sign, skip, first in signs:
        coming[sign] = [
            link.copy(shard(4, skip, half), slot(first, half), device(2 * sign)),
            link.copy(shard(3 * sign, 0, size), slot(first + 1, size), device(sign)),
        ]
    for sign, skip, first in signs:
        straight.append(link.copy(shard(sign, 0, size), slot(first + 2, size), device(sign)))
    yield
    for sign, skip, first in signs:
        take(coming[sign])
        target = shard(2 * sign, 0, size)
        target[...] = target[...] + slot(first + 1, size)[...]
        part = shard(2 * sign, skip, half)
        part[...] = part[...] + slot(first, half)[...]
        joined.append(link.copy(target, slot(first + 3, size), device(2 * sign)))
    yield
    take(straight)
    take(joined)
    total = shard(0, 0, size)[...]
    for index in (2, 3, 6, 7):
        total = total + slot(index, size)[...]
    rows(into, base + at * size, size)[...] = total


def gather_pair_steps(link, into, base, at, n, size, device):
    half = size // 2

    def shard(offset, skip=0, extent=size):
        return rows(into, base + lax.rem(at + offset + n, n) * size + skip, extent)

    signs = ((1, 0), (-1, half))
    far = {sign: link.copy(shard(0), shard(0), device(2 * sign)) for sign, skip in signs}
    near = [link.copy(shard(0), shard(0), device(sign)) for sign, skip in signs]
    yield
    last = []
    for sign, skip in signs:
        far[sign].wait_recv()
        passed = shard(-2 * sign, skip, half)
        last.append(link.copy(passed, passed, device(2 * sign)))
        passed = shard(-2 * sign)
        last.append(link.copy(passed, passed, device(sign)))
    yield
    take(near)
    take(last)


def feat_total(link, place, work, into, near, slots, extent):
    half = extent // 2
    quarter = half // NX
    x, mine, other = place["x"], place["core"] * half, (1 - place["core"]) * half
    pairs = {}
    for offset in FAR_FIRST[NX] + (0,):
        start = lax.rem(x + offset, NX) * quarter
        pairs[offset] = (
            start,
            link.copy(rows(work, other + start, quarter), rows(near, start, quarter), place["partner"]),
        )
    yield

    def ready(offset):
        start, copy = pairs[offset]
        copy.wait_recv()
        target = rows(work, mine + start, quarter)
        target[...] = target[...] + rows(near, start, quarter)[...]

    yield from reduce_direct(
        link, work, into, mine, x, NX, quarter, place["along_x"], slots, ready
    )
    shared = []

    def also(ref):
        shared.append(link.copy(ref, ref, place["partner"]))

    yield from gather_direct(link, into, mine, x, NX, quarter, place["along_x"], also)
    yield
    take(shared)


def upper_total(link, place, work, into, slots, base, extent):
    y, z = place["y"], place["z"]
    size, small = extent // NY, extent // NY // NZ
    near = base + y * size
    along_y, along_z = place["along_y"], place["along_z"]
    yield from reduce_direct(link, work, work, base, y, NY, size, along_y, rows(slots, 0, extent))
    yield from reduce_direct(link, work, into, near, z, NZ, small, along_z, rows(slots, extent, size))
    yield from gather_direct(link, into, near, z, NZ, small, along_z)
    yield from gather_direct(link, into, base, y, NY, size, along_y)


def lower_total(link, place, work, into, slots, base, extent):
    y, z = place["y"], place["z"]
    size, small = extent // NZ, extent // NZ // NY
    near = base + z * size
    along_y, along_z = place["along_y"], place["along_z"]
    yield from reduce_pair_steps(link, work, work, base, z, NZ, size, along_z, rows(slots, 0, extent))
    yield from reduce_direct(link, work, into, near, y, NY, small, along_y, rows(slots, extent, size))
    yield from gather_direct(link, into, near, y, NY, small, along_y)
    yield from gather_pair_steps(link, into, base, z, NZ, size, along_z)


def run(*streams):
    streams = list(streams)
    while streams:
        for stream in list(streams):
            try:
                next(stream)
            except StopIteration:
                streams.remove(stream)


def halves(value):
    high = value.astype(BF)
    return high, (value - high.astype(F32)).astype(BF)


def dot(left, right, dims=(((1,), (0,)), ((), ()))):
    return lax.dot_general(left, right, dims, preferred_element_type=F32)


def product(left, right, dims=(((1,), (0,)), ((), ()))):
    (lh, ll), (rh, rl) = left, right
    return dot(lh, rh, dims) + (dot(lh, rl, dims) + dot(ll, rh, dims))


def times(left, right):
    return product(halves(left), halves(right))


def inverse_root(total):
    guess = lax.rsqrt(total)
    return guess * (1.5 - 0.5 * total * guess * guess)


def diagonal(p):
    return lax.broadcasted_iota(jnp.int32, (p, p), 0) == lax.broadcasted_iota(jnp.int32, (p, p), 1)


def root_of_trace(gram):
    total = jnp.sum(jnp.where(diagonal(gram.shape[0]), gram, 0.0), keepdims=True)
    return inverse_root(total)


def newton(gram, step, turn):
    p = gram.shape[0]
    for at in range(NS_STEPS):
        step[...] = jnp.where(diagonal(p), 1.5, 0.0) - 0.5 * gram[...]
        if at == 0:
            turn[...] = step[...]
        else:
            turn[...] = times(turn[...], step[...])
        if at + 1 < NS_STEPS:
            yield
            gram[...] = times(gram[...], step[...])
            yield
            gram[...] = times(gram[...], step[...])
            yield


def kernel(
    ranks, b_hbm, a_hbm, p_hbm, out,
    stage, b_stage, a_high, a_low, b_high, b_low, y_high, y_low, c_high, c_low,
    work_a, into_a, near_a, slots_a,
    work_b, into_b, near_b, slots_b,
    work_g, into_g, near_g, slots_g,
    work_h, into_h, near_h, slots_h,
    panel_one, panel_two, whole_one, whole_two, rings_one, rings_two,
    probe, gram, step, turn_one, turn_two,
    send, recv, local,
):
    clients, features, rank = b_hbm.shape
    p = probe.shape[1]
    slots = clients * rank
    cohort, feat = lax.axis_index("cohort"), lax.axis_index("feat")
    z, y = lax.div(cohort, NY), lax.rem(cohort, NY)
    x, core = lax.div(feat, 2), lax.rem(feat, 2)
    place = {
        "x": x, "y": y, "z": z, "core": core,
        "partner": (cohort, x * 2 + 1 - core),
        "along_x": lambda d: (cohort, lax.rem(x + d + NX, NX) * 2 + core),
        "along_y": lambda d: (z * NY + lax.rem(y + d + NY, NY), feat),
        "along_z": lambda d: (lax.rem(z + d + NZ, NZ) * NY + y, feat),
    }
    peers = [place["partner"]]
    for axis, n in (("along_x", NX), ("along_y", NY), ("along_z", NZ)):
        peers += [place[axis](d) for d in range(1, n)]

    def load(source, into, c, sem):
        start = pl.multiple_of(c * rank, rank)
        across = into is b_stage
        target = into.at[:, pl.ds(start, rank)] if across else into.at[pl.ds(start, rank), :]
        return pltpu.make_async_copy(source.at[c], target, local.at[sem])

    core, pairs = place["core"], clients // 2
    wanted = [2 * k + 1 - core for k in range(pairs)] + [2 * k + core for k in range(pairs)]
    load_p = pltpu.make_async_copy(p_hbm, probe, local.at[0])
    load_p.start()
    load_a = [load(a_hbm, stage, c, 1 + k) for k, c in enumerate(wanted)]
    load_b = [load(b_hbm, b_stage, c, 1 + clients + c) for c in range(clients)]
    for copy in load_a:
        copy.start()

    barrier = pltpu.get_barrier_semaphore()
    for peer in peers:
        pl.semaphore_signal(barrier, inc=1, device_id=peer, device_id_type=MESH)

    link = Link(send, recv)
    load_p.wait()
    y_high[...], y_low[...] = halves(probe[...])

    def client_coef(work, c):
        at = pl.ds(pl.multiple_of(c * rank, rank), rank)
        total = product((a_high[at, :], a_low[at, :]), (y_high[...], y_low[...]))
        live = lax.broadcasted_iota(jnp.int32, total.shape, 0) < ranks[c]
        work[at, :] = jnp.where(live, total, 0.0)

    def feat_stream(spaces, k, extent):
        work, into, near, slot_rows = spaces
        return feat_total(
            link, place, rows(work, k * extent, extent), rows(into, k * extent, extent),
            rows(near, k * extent // 2, extent // 2), rows(slot_rows, k * extent // 2, extent // 2),
            extent,
        )

    def coef_total(spaces, fetch, *others):
        streams = [feat_stream(spaces, k, 2 * rank) for k in range(pairs)]
        for k, c in enumerate(wanted):
            fetch(k, c)
            client_coef(spaces[0], c)
            if k < pairs:
                if k == 0 and fetch is first_fetch:
                    pl.semaphore_wait(barrier, len(peers))
                next(streams[k])
        run(*streams, *others)

    def first_fetch(k, c):
        load_a[k].wait()
        at = pl.ds(pl.multiple_of(c * rank, rank), rank)
        a_high[at, :], a_low[at, :] = halves(stage[at, :])
        if k == pairs - 1:
            for copy in load_b:
                copy.start()

    def b_stream():
        for c in range(clients):
            load_b[c].wait()
            across = pl.ds(c * rank, rank)
            for k in range(2):
                at = pl.ds(k * (features // 2), features // 2)
                b_high[at, across], b_low[at, across] = halves(b_stage[at, across])
            yield

    def panel_total(work, into, rings, *others):
        part = features // 4
        streams = []
        for k, kind in enumerate((lower_total, lower_total, upper_total, upper_total)):
            at = pl.ds(k * part, part)
            work[at, :] = product((b_high[at, :], b_low[at, :]), (c_high[...], c_low[...]))
            streams.append(
                kind(link, place, work, into, rows(rings, 2 * k * part, 2 * part), k * part, part)
            )
            next(streams[k])
        for kind in (0, 1, 0, 1, 0, 0, 1, 0, 1, 0):
            for stream in streams[2 * kind:2 * kind + 2]:
                for other in others:
                    next(other, None)
                next(stream, None)
        run(*others)

    spaces_a = (work_a, into_a, near_a, slots_a)
    spaces_b = (work_b, into_b, near_b, slots_b)
    spaces_g = (work_g, into_g, near_g, slots_g)
    spaces_h = (work_h, into_h, near_h, slots_h)
    contract_rows = (((0,), (0,)), ((), ()))

    def local_gram(work):
        work[...] = product(
            (y_high[...], y_low[...]), (y_high[...], y_low[...]), contract_rows
        )

    def gram_total(spaces):
        local_gram(spaces[0])
        yield from feat_stream(spaces, 0, p)

    coef_total(spaces_a, first_fetch, b_stream())
    c_high[...], c_low[...] = halves(into_a[...])
    panel_total(panel_one, whole_one, rings_one)
    link.drain()

    y_high[...], y_low[...] = halves(whole_one[...])
    coef_total(spaces_b, lambda k, c: None, gram_total(spaces_g))
    gram[...] = into_g[...]
    scale = root_of_trace(gram[...])
    gram[...] = gram[...] * (scale * scale)
    c_high[...], c_low[...] = halves(into_b[...] * scale)
    panel_total(panel_two, whole_two, rings_two, newton(gram, step, turn_one))

    y_high[...], y_low[...] = halves(whole_two[...])
    run(gram_total(spaces_h))
    gram[...] = times(times(turn_one[...], into_h[...]), turn_one[...])
    scale = root_of_trace(gram[...])
    gram[...] = gram[...] * (scale * scale)
    run(newton(gram, step, turn_two))
    last = times(turn_one[...], turn_two[...]) * (scale * math.sqrt(D))
    out[...] = product((y_high[...], y_low[...]), halves(last))
    link.drain()


def on_device(b_factors, a_factors, ranks, probes):
    clients, features, rank = b_factors.shape
    p = probes.shape[1]
    slots = clients * rank
    vm = pltpu.VMEM

    def feat_space(extent):
        return [
            vm((extent, p), F32), vm((extent, p), F32), vm((extent // 2, p), F32),
            vm((extent // 2, p), F32),
        ]

    scratch = (
        [vm((slots, features), F32), vm((features, slots), F32)]
        + [vm((slots, features), BF)] * 2
        + [vm((features, slots), BF)] * 2
        + [vm((features, p), BF)] * 2
        + [vm((slots, p), BF)] * 2
        + feat_space(slots) * 2 + feat_space(p) * 2
        + [vm((features, p), F32)] * 4
        + [vm((2 * features, p), F32)] * 2
        + [vm((features, p), F32)]
        + [vm((p, p), F32)] * 4
        + [pltpu.SemaphoreType.DMA((260,)), pltpu.SemaphoreType.DMA((260,)), pltpu.SemaphoreType.DMA((1 + 2 * clients,))]
    )
    anywhere = pl.BlockSpec(memory_space=pl.ANY)
    return pl.pallas_call(
        kernel,
        out_shape=jax.ShapeDtypeStruct((features, p), F32),
        in_specs=[pl.BlockSpec(memory_space=pltpu.SMEM), anywhere, anywhere, anywhere],
        out_specs=pl.BlockSpec(memory_space=pltpu.VMEM),
        scratch_shapes=scratch,
        compiler_params=pltpu.CompilerParams(
            collective_id=0, has_side_effects=True, vmem_limit_bytes=60 << 20
        ),
    )(ranks, b_factors, a_factors, probes)


def solution(mesh):
    in_specs = (P("cohort", "feat", None), P("cohort", None, "feat"), P("cohort"), P("feat", None))
    out_specs = P("feat", None)
    return jax.shard_map(
        on_device, mesh=mesh, in_specs=in_specs, out_specs=out_specs, check_vma=False
    )
```

```python
import functools
import math

import jax
import jax.numpy as jnp
from jax import lax
from jax.experimental import pallas as pl
from jax.experimental.pallas import tpu as pltpu
from jax.sharding import PartitionSpec as P

D = 8192
NS_STEPS = 5
NX, NY, NZ = 4, 4, 8
MESH = pl.DeviceIdType.MESH
FAR_FIRST = {4: (2, 1, 3), 8: (4, 3, 5, 2, 6, 1, 7)}
BF = jnp.bfloat16
F32 = jnp.float32


def rows(ref, start, size):
    if not isinstance(start, int):
        start = pl.multiple_of(start, 8)
    return ref.at[pl.ds(start, size), :]


class Link:
    def __init__(self, send, recv):
        self.send, self.recv, self.count, self.sent = send, recv, 0, []

    def copy(self, src, dst, device):
        copy = pltpu.make_async_remote_copy(
            src_ref=src,
            dst_ref=dst,
            send_sem=self.send.at[self.count],
            recv_sem=self.recv.at[self.count],
            device_id=device,
            device_id_type=MESH,
        )
        copy.start()
        self.count += 1
        self.sent.append(copy)
        return copy

    def drain(self):
        for copy in self.sent:
            copy.wait_send()
        self.sent = []


def take(copies):
    for copy in copies:
        copy.wait_recv()


def reduce_direct(link, work, into, base, at, n, size, device, slots, ready=None):
    coming = []
    for offset in FAR_FIRST[n]:
        start = base + lax.rem(at + offset, n) * size
        if ready is not None:
            ready(offset)
        coming.append(
            link.copy(
                rows(work, start, size), rows(slots, (offset - 1) * size, size), device(offset)
            )
        )
    if ready is not None:
        ready(0)
    yield
    take(coming)
    total = rows(work, base + at * size, size)[...]
    for step in range(n - 1):
        total = total + rows(slots, step * size, size)[...]
    rows(into, base + at * size, size)[...] = total


def gather_direct(link, into, base, at, n, size, device, also=None):
    own = rows(into, base + at * size, size)
    coming = [(offset, link.copy(own, own, device(offset))) for offset in FAR_FIRST[n]]
    if also is not None:
        also(own)
    yield
    for offset, copy in reversed(coming):
        copy.wait_recv()
        if also is not None:
            also(rows(into, base + lax.rem(at + n - offset, n) * size, size))


def reduce_pair_steps(link, work, into, base, at, n, size, device, slots):
    half = size // 2

    def shard(offset, skip, extent):
        return rows(work, base + lax.rem(at + offset + n, n) * size + skip, extent)

    def slot(index, extent):
        return rows(slots, index * size, extent)

    signs = ((1, 0, 0), (-1, half, 4))
    coming, straight, joined = {}, [], []
    for sign, skip, first in signs:
        coming[sign] = [
            link.copy(shard(4, skip, half), slot(first, half), device(2 * sign)),
            link.copy(shard(3 * sign, 0, size), slot(first + 1, size), device(sign)),
        ]
    for sign, skip, first in signs:
        straight.append(link.copy(shard(sign, 0, size), slot(first + 2, size), device(sign)))
    yield
    for sign, skip, first in signs:
        take(coming[sign])
        target = shard(2 * sign, 0, size)
        target[...] = target[...] + slot(first + 1, size)[...]
        part = shard(2 * sign, skip, half)
        part[...] = part[...] + slot(first, half)[...]
        joined.append(link.copy(target, slot(first + 3, size), device(2 * sign)))
    yield
    take(straight)
    take(joined)
    total = shard(0, 0, size)[...]
    for index in (2, 3, 6, 7):
        total = total + slot(index, size)[...]
    rows(into, base + at * size, size)[...] = total


def gather_pair_steps(link, into, base, at, n, size, device):
    half = size // 2

    def shard(offset, skip=0, extent=size):
        return rows(into, base + lax.rem(at + offset + n, n) * size + skip, extent)

    signs = ((1, 0), (-1, half))
    far = {sign: link.copy(shard(0), shard(0), device(2 * sign)) for sign, skip in signs}
    near = [link.copy(shard(0), shard(0), device(sign)) for sign, skip in signs]
    yield
    last = []
    for sign, skip in signs:
        far[sign].wait_recv()
        passed = shard(-2 * sign, skip, half)
        last.append(link.copy(passed, passed, device(2 * sign)))
        passed = shard(-2 * sign)
        last.append(link.copy(passed, passed, device(sign)))
    yield
    take(near)
    take(last)


def feat_total(link, place, work, into, near, slots, extent):
    half = extent // 2
    quarter = half // NX
    x, mine, other = place["x"], place["core"] * half, (1 - place["core"]) * half
    pairs = {}
    for offset in FAR_FIRST[NX] + (0,):
        start = lax.rem(x + offset, NX) * quarter
        pairs[offset] = (
            start,
            link.copy(rows(work, other + start, quarter), rows(near, start, quarter), place["partner"]),
        )
    yield

    def ready(offset):
        start, copy = pairs[offset]
        copy.wait_recv()
        target = rows(work, mine + start, quarter)
        target[...] = target[...] + rows(near, start, quarter)[...]

    yield from reduce_direct(
        link, work, into, mine, x, NX, quarter, place["along_x"], slots, ready
    )
    shared = []

    def also(ref):
        shared.append(link.copy(ref, ref, place["partner"]))

    yield from gather_direct(link, into, mine, x, NX, quarter, place["along_x"], also)
    yield
    take(shared)


def upper_total(link, place, work, into, slots, base, extent):
    y, z = place["y"], place["z"]
    size, small = extent // NY, extent // NY // NZ
    near = base + y * size
    along_y, along_z = place["along_y"], place["along_z"]
    yield from reduce_direct(link, work, work, base, y, NY, size, along_y, rows(slots, 0, extent))
    yield from reduce_direct(link, work, into, near, z, NZ, small, along_z, rows(slots, extent, size))
    yield from gather_direct(link, into, near, z, NZ, small, along_z)
    yield from gather_direct(link, into, base, y, NY, size, along_y)


def lower_total(link, place, work, into, slots, base, extent):
    y, z = place["y"], place["z"]
    size, small = extent // NZ, extent // NZ // NY
    near = base + z * size
    along_y, along_z = place["along_y"], place["along_z"]
    yield from reduce_pair_steps(link, work, work, base, z, NZ, size, along_z, rows(slots, 0, extent))
    yield from reduce_direct(link, work, into, near, y, NY, small, along_y, rows(slots, extent, size))
    yield from gather_direct(link, into, near, y, NY, small, along_y)
    yield from gather_pair_steps(link, into, base, z, NZ, size, along_z)


def run(*streams):
    streams = list(streams)
    while streams:
        for stream in list(streams):
            try:
                next(stream)
            except StopIteration:
                streams.remove(stream)


def halves(value):
    high = value.astype(BF)
    return high, (value - high.astype(F32)).astype(BF)


def dot(left, right, dims=(((1,), (0,)), ((), ()))):
    return lax.dot_general(left, right, dims, preferred_element_type=F32)


def product(left, right, dims=(((1,), (0,)), ((), ()))):
    (lh, ll), (rh, rl) = left, right
    return dot(lh, rh, dims) + (dot(lh, rl, dims) + dot(ll, rh, dims))


def times(left, right):
    return product(halves(left), halves(right))


def inverse_root(total):
    guess = lax.rsqrt(total)
    return guess * (1.5 - 0.5 * total * guess * guess)


def diagonal(p):
    return lax.broadcasted_iota(jnp.int32, (p, p), 0) == lax.broadcasted_iota(jnp.int32, (p, p), 1)


def root_of_trace(gram):
    total = jnp.sum(jnp.where(diagonal(gram.shape[0]), gram, 0.0), keepdims=True)
    return inverse_root(total)


def newton(gram, step, turn):
    p = gram.shape[0]
    for at in range(NS_STEPS):
        step[...] = jnp.where(diagonal(p), 1.5, 0.0) - 0.5 * gram[...]
        if at == 0:
            turn[...] = step[...]
        else:
            turn[...] = times(turn[...], step[...])
        if at + 1 < NS_STEPS:
            yield
            gram[...] = times(gram[...], step[...])
            yield
            gram[...] = times(gram[...], step[...])
            yield


def kernel(
    ranks, b_hbm, a_hbm, p_hbm, out,
    stage, b_stage, a_high, a_low, b_high, b_low, y_high, y_low, c_high, c_low,
    work_a, into_a, near_a, slots_a,
    work_b, into_b, near_b, slots_b,
    work_g, into_g, slots_g, work_h, into_h, slots_h, marks,
    panel_one, panel_two, whole_one, whole_two, rings_one, rings_two,
    probe, gram, step, turn_one, turn_two,
    send, recv, local,
):
    clients, features, rank = b_hbm.shape
    p = probe.shape[1]
    slots = clients * rank
    cohort, feat = lax.axis_index("cohort"), lax.axis_index("feat")
    z, y = lax.div(cohort, NY), lax.rem(cohort, NY)
    x, core = lax.div(feat, 2), lax.rem(feat, 2)
    place = {
        "x": x, "y": y, "z": z, "core": core,
        "partner": (cohort, x * 2 + 1 - core),
        "feat": feat,
        "along_feat": lambda d: (cohort, lax.rem(feat + d, 2 * NX)),
        "along_x": lambda d: (cohort, lax.rem(x + d + NX, NX) * 2 + core),
        "along_y": lambda d: (z * NY + lax.rem(y + d + NY, NY), feat),
        "along_z": lambda d: (lax.rem(z + d + NZ, NZ) * NY + y, feat),
    }
    peers = []
    for axis, n in (("along_feat", 2 * NX), ("along_y", NY), ("along_z", NZ)):
        peers += [place[axis](d) for d in range(1, n)]

    def load(source, into, c, sem):
        start = pl.multiple_of(c * rank, rank)
        across = into is b_stage
        target = into.at[:, pl.ds(start, rank)] if across else into.at[pl.ds(start, rank), :]
        return pltpu.make_async_copy(source.at[c], target, local.at[sem])

    core, pairs = place["core"], clients // 2
    wanted = [2 * k + 1 - core for k in range(pairs)] + [2 * k + core for k in range(pairs)]
    load_p = pltpu.make_async_copy(p_hbm, probe, local.at[0])
    load_p.start()
    load_a = [load(a_hbm, stage, c, 1 + k) for k, c in enumerate(wanted)]
    load_b = [load(b_hbm, b_stage, c, 1 + clients + c) for c in range(clients)]
    for copy in load_a:
        copy.start()

    barrier = pltpu.get_barrier_semaphore()
    for peer in peers:
        pl.semaphore_signal(barrier, inc=1, device_id=peer, device_id_type=MESH)

    link = Link(send, recv)
    load_p.wait()
    y_high[...], y_low[...] = halves(probe[...])

    def client_coef(work, c, start, extent, begin, end):
        at, part = pl.ds(pl.multiple_of(c * rank, rank), rank), pl.ds(start, extent)
        total = product((a_high[at, part], a_low[at, part]), (y_high[part, :], y_low[part, :]))
        if not begin:
            total = total + work[at, :]
        if end:
            live = lax.broadcasted_iota(jnp.int32, total.shape, 0) < ranks[c]
            total = jnp.where(live, total, 0.0)
        work[at, :] = total

    def feat_stream(spaces, k, extent):
        work, into, near, slot_rows = spaces
        return feat_total(
            link, place, rows(work, k * extent, extent), rows(into, k * extent, extent),
            rows(near, k * extent // 2, extent // 2), rows(slot_rows, k * extent // 2, extent // 2),
            extent,
        )

    def coef_total(spaces, coef, *others):
        streams = [feat_stream(spaces, k, 2 * rank) for k in range(pairs)]
        for k, c in enumerate(wanted):
            coef(k, c)
            if k < pairs:
                next(streams[k])
        run(*streams, *others)

    def first_coef(k, c):
        load_a[k].wait()
        at = pl.ds(pl.multiple_of(c * rank, rank), rank)
        a_high[at, :], a_low[at, :] = halves(stage[at, :])
        if k == pairs - 1:
            for copy in load_b:
                copy.start()
        client_coef(work_a, c, 0, features, True, True)
        if k == 0:
            pl.semaphore_wait(barrier, len(peers))

    def b_stream():
        for c in range(clients):
            load_b[c].wait()
            across = pl.ds(c * rank, rank)
            for k in range(2):
                at = pl.ds(k * (features // 2), features // 2)
                b_high[at, across], b_low[at, across] = halves(b_stage[at, across])
            yield

    part = features // 4

    def panel_total(work, into, rings, done, *others):
        streams, open_streams = [], set(range(4))
        for k, kind in enumerate((lower_total, lower_total, upper_total, upper_total)):
            at = pl.ds(k * part, part)
            work[at, :] = product((b_high[at, :], b_low[at, :]), (c_high[...], c_low[...]))
            streams.append(
                kind(link, place, work, into, rows(rings, 2 * k * part, 2 * part), k * part, part)
            )
            next(streams[k])
        for kind in (0, 1, 0, 1, 0, 0, 1, 0, 1, 0):
            for k in (2 * kind, 2 * kind + 1):
                for other in others:
                    next(other, None)
                if k in open_streams and next(streams[k], part) == part:
                    open_streams.remove(k)
                    done(k, len(open_streams))
        run(*others)

    spaces_a = (work_a, into_a, near_a, slots_a)
    spaces_b = (work_b, into_b, near_b, slots_b)
    contract_rows = (((0,), (0,)), ((), ()))

    def split_rows(whole, k):
        at = pl.ds(k * part, part)
        y_high[at, :], y_low[at, :] = halves(whole[at, :])
        return at

    def add_gram(work, at, begin):
        value = (y_high[at, :], y_low[at, :])
        total = product(value, value, contract_rows)
        work[...] = total if begin else work[...] + total

    def gram_total(work, into, slot_rows):
        each = p // (2 * NX)
        ring = (place["feat"], 2 * NX, each, place["along_feat"])
        yield from reduce_direct(link, work, into, 0, *ring, slot_rows)
        yield from gather_direct(link, into, 0, *ring)

    def trace_total():
        square = whole_one[...] * whole_one[...]
        own = pl.ds(pl.multiple_of(place["feat"] * 8, 8), 8)
        marks[own, :] = jnp.sum(square.reshape(features // 8, 8, p), axis=0)
        yield from gather_direct(link, marks, 0, place["feat"], 2 * NX, 8, place["along_feat"])

    coef_total(spaces_a, first_coef, b_stream())
    c_high[...], c_low[...] = halves(into_a[...])

    last_part = []

    def first_done(k, left):
        at = split_rows(whole_one, k)
        if left:
            for c in range(clients):
                client_coef(work_b, c, k * part, part, left == 3, False)
        else:
            last_part.append(k * part)

    panel_total(panel_one, whole_one, rings_one, first_done)
    link.drain()

    coef_total(
        spaces_b, lambda k, c: client_coef(work_b, c, last_part[0], part, False, True), trace_total()
    )
    scale_one = inverse_root(jnp.sum(marks[...], keepdims=True))
    c_high[...], c_low[...] = halves(into_b[...] * scale_one)

    def first_turn():
        for k in range(4):
            add_gram(work_g, pl.ds(k * part, part), k == 0)
        yield from gram_total(work_g, into_g, slots_g)
        gram[...] = into_g[...] * (scale_one * scale_one)
        yield from newton(gram, step, turn_one)

    def second_done(k, left):
        add_gram(work_h, split_rows(whole_two, k), left == 3)

    panel_total(panel_two, whole_two, rings_two, second_done, first_turn())

    run(gram_total(work_h, into_h, slots_h))
    gram[...] = times(times(turn_one[...], into_h[...]), turn_one[...])
    scale = root_of_trace(gram[...])
    gram[...] = gram[...] * (scale * scale)
    run(newton(gram, step, turn_two))
    last = times(turn_one[...], turn_two[...]) * (scale * math.sqrt(D))
    out[...] = product((y_high[...], y_low[...]), halves(last))
    link.drain()


def on_device(b_factors, a_factors, ranks, probes):
    clients, features, rank = b_factors.shape
    p = probes.shape[1]
    slots = clients * rank
    vm = pltpu.VMEM

    def feat_space(extent):
        return [
            vm((extent, p), F32), vm((extent, p), F32), vm((extent // 2, p), F32),
            vm((extent // 2, p), F32),
        ]

    scratch = (
        [vm((slots, features), F32), vm((features, slots), F32)]
        + [vm((slots, features), BF)] * 2
        + [vm((features, slots), BF)] * 2
        + [vm((features, p), BF)] * 2
        + [vm((slots, p), BF)] * 2
        + feat_space(slots) * 2 + [vm((p, p), F32)] * 6 + [vm((16 * NX, p), F32)]
        + [vm((features, p), F32)] * 4
        + [vm((2 * features, p), F32)] * 2
        + [vm((features, p), F32)]
        + [vm((p, p), F32)] * 4
        + [pltpu.SemaphoreType.DMA((280,)), pltpu.SemaphoreType.DMA((280,)), pltpu.SemaphoreType.DMA((1 + 2 * clients,))]
    )
    anywhere = pl.BlockSpec(memory_space=pltpu.MemorySpace.HBM)
    return pl.pallas_call(
        kernel,
        out_shape=jax.ShapeDtypeStruct((features, p), F32),
        in_specs=[pl.BlockSpec(memory_space=pltpu.SMEM), anywhere, anywhere, anywhere],
        out_specs=pl.BlockSpec(memory_space=pltpu.VMEM),
        scratch_shapes=scratch,
        compiler_params=pltpu.CompilerParams(
            collective_id=0, has_side_effects=True, vmem_limit_bytes=52 << 20
        ),
    )(ranks, b_factors, a_factors, probes)


def solution(mesh):
    in_specs = (P("cohort", "feat", None), P("cohort", None, "feat"), P("cohort"), P("feat", None))
    out_specs = P("feat", None)
    return jax.shard_map(
        on_device, mesh=mesh, in_specs=in_specs, out_specs=out_specs, check_vma=False
    )
```

```python
import functools
import math

import jax
import jax.numpy as jnp
from jax import lax
from jax.experimental import pallas as pl
from jax.experimental.pallas import tpu as pltpu
from jax.sharding import PartitionSpec as P

D = 8192
NS_STEPS = 5
NX, NY, NZ = 4, 4, 8
MESH = pl.DeviceIdType.MESH
FAR_FIRST = {4: (2, 1, 3), 8: (4, 3, 5, 2, 6, 1, 7)}
BF = jnp.bfloat16
F32 = jnp.float32


def rows(ref, start, size):
    if not isinstance(start, int):
        start = pl.multiple_of(start, 8)
    return ref.at[pl.ds(start, size), :]


class Link:
    def __init__(self, send, recv):
        self.send, self.recv, self.count, self.sent = send, recv, 0, []

    def copy(self, src, dst, device):
        copy = pltpu.make_async_remote_copy(
            src_ref=src,
            dst_ref=dst,
            send_sem=self.send.at[self.count],
            recv_sem=self.recv.at[self.count],
            device_id=device,
            device_id_type=MESH,
        )
        copy.start()
        self.count += 1
        self.sent.append(copy)
        return copy

    def drain(self):
        for copy in self.sent:
            copy.wait_send()
        self.sent = []


def take(copies):
    for copy in copies:
        copy.wait_recv()


def reduce_direct(link, work, into, base, at, n, size, device, slots, ready=None):
    coming = []
    for offset in FAR_FIRST[n]:
        start = base + lax.rem(at + offset, n) * size
        if ready is not None:
            ready(offset)
        coming.append(
            link.copy(
                rows(work, start, size), rows(slots, (offset - 1) * size, size), device(offset)
            )
        )
    if ready is not None:
        ready(0)
    yield
    take(coming)
    total = rows(work, base + at * size, size)[...]
    for step in range(n - 1):
        total = total + rows(slots, step * size, size)[...]
    rows(into, base + at * size, size)[...] = total


def gather_direct(link, into, base, at, n, size, device, also=None):
    own = rows(into, base + at * size, size)
    coming = [(offset, link.copy(own, own, device(offset))) for offset in FAR_FIRST[n]]
    if also is not None:
        also(own)
    yield
    for offset, copy in reversed(coming):
        copy.wait_recv()
        if also is not None:
            also(rows(into, base + lax.rem(at + n - offset, n) * size, size))


def reduce_pair_steps(link, work, into, base, at, n, size, device, slots):
    half = size // 2

    def shard(offset, skip, extent):
        return rows(work, base + lax.rem(at + offset + n, n) * size + skip, extent)

    def slot(index, extent):
        return rows(slots, index * size, extent)

    signs = ((1, 0, 0), (-1, half, 4))
    coming, straight, joined = {}, [], []
    for sign, skip, first in signs:
        coming[sign] = [
            link.copy(shard(4, skip, half), slot(first, half), device(2 * sign)),
            link.copy(shard(3 * sign, 0, size), slot(first + 1, size), device(sign)),
        ]
    for sign, skip, first in signs:
        straight.append(link.copy(shard(sign, 0, size), slot(first + 2, size), device(sign)))
    yield
    for sign, skip, first in signs:
        take(coming[sign])
        target = shard(2 * sign, 0, size)
        target[...] = target[...] + slot(first + 1, size)[...]
        part = shard(2 * sign, skip, half)
        part[...] = part[...] + slot(first, half)[...]
        joined.append(link.copy(target, slot(first + 3, size), device(2 * sign)))
    yield
    take(straight)
    take(joined)
    total = shard(0, 0, size)[...]
    for index in (2, 3, 6, 7):
        total = total + slot(index, size)[...]
    rows(into, base + at * size, size)[...] = total


def gather_pair_steps(link, into, base, at, n, size, device):
    half = size // 2

    def shard(offset, skip=0, extent=size):
        return rows(into, base + lax.rem(at + offset + n, n) * size + skip, extent)

    signs = ((1, 0), (-1, half))
    far = {sign: link.copy(shard(0), shard(0), device(2 * sign)) for sign, skip in signs}
    near = [link.copy(shard(0), shard(0), device(sign)) for sign, skip in signs]
    yield
    last = []
    for sign, skip in signs:
        far[sign].wait_recv()
        passed = shard(-2 * sign, skip, half)
        last.append(link.copy(passed, passed, device(2 * sign)))
        passed = shard(-2 * sign)
        last.append(link.copy(passed, passed, device(sign)))
    yield
    take(near)
    take(last)


def feat_total(link, place, work, into, near, slots, extent):
    half = extent // 2
    quarter = half // NX
    x, mine, other = place["x"], place["core"] * half, (1 - place["core"]) * half
    pairs = {}
    for offset in FAR_FIRST[NX] + (0,):
        start = lax.rem(x + offset, NX) * quarter
        pairs[offset] = (
            start,
            link.copy(rows(work, other + start, quarter), rows(near, start, quarter), place["partner"]),
        )
    yield

    def ready(offset):
        start, copy = pairs[offset]
        copy.wait_recv()
        target = rows(work, mine + start, quarter)
        target[...] = target[...] + rows(near, start, quarter)[...]

    yield from reduce_direct(
        link, work, into, mine, x, NX, quarter, place["along_x"], slots, ready
    )
    shared = []

    def also(ref):
        shared.append(link.copy(ref, ref, place["partner"]))

    yield from gather_direct(link, into, mine, x, NX, quarter, place["along_x"], also)
    yield
    take(shared)


def upper_total(link, place, work, into, slots, base, extent):
    y, z = place["y"], place["z"]
    size, small = extent // NY, extent // NY // NZ
    near = base + y * size
    along_y, along_z = place["along_y"], place["along_z"]
    yield from reduce_direct(link, work, work, base, y, NY, size, along_y, rows(slots, 0, extent))
    yield from reduce_direct(link, work, into, near, z, NZ, small, along_z, rows(slots, extent, size))
    yield from gather_direct(link, into, near, z, NZ, small, along_z)
    yield from gather_direct(link, into, base, y, NY, size, along_y)


def lower_total(link, place, work, into, slots, base, extent):
    y, z = place["y"], place["z"]
    size, small = extent // NZ, extent // NZ // NY
    near = base + z * size
    along_y, along_z = place["along_y"], place["along_z"]
    yield from reduce_pair_steps(link, work, work, base, z, NZ, size, along_z, rows(slots, 0, extent))
    yield from reduce_direct(link, work, into, near, y, NY, small, along_y, rows(slots, extent, size))
    yield from gather_direct(link, into, near, y, NY, small, along_y)
    yield from gather_pair_steps(link, into, base, z, NZ, size, along_z)


def run(*streams):
    streams = list(streams)
    while streams:
        for stream in list(streams):
            try:
                next(stream)
            except StopIteration:
                streams.remove(stream)


def halves(value):
    high = value.astype(BF)
    return high, (value - high.astype(F32)).astype(BF)


def dot(left, right, dims=(((1,), (0,)), ((), ()))):
    return lax.dot_general(left, right, dims, preferred_element_type=F32)


def product(left, right, dims=(((1,), (0,)), ((), ()))):
    (lh, ll), (rh, rl) = left, right
    return dot(lh, rh, dims) + (dot(lh, rl, dims) + dot(ll, rh, dims))


def times(left, right):
    return product(halves(left), halves(right))


def inverse_root(total):
    guess = lax.rsqrt(total)
    return guess * (1.5 - 0.5 * total * guess * guess)


def diagonal(p):
    return lax.broadcasted_iota(jnp.int32, (p, p), 0) == lax.broadcasted_iota(jnp.int32, (p, p), 1)


def root_of_trace(gram):
    total = jnp.sum(jnp.where(diagonal(gram.shape[0]), gram, 0.0), keepdims=True)
    return inverse_root(total)


def newton(gram, turn):
    for at in range(NS_STEPS):
        step = jnp.where(diagonal(gram.shape[0]), 1.5, 0.0) - 0.5 * gram[...]
        split = halves(step)
        turn[...] = step if at == 0 else product(halves(turn[...]), split)
        if at + 1 < NS_STEPS:
            for factor in range(2):
                yield
                gram[...] = product(halves(gram[...]), split)
            yield


def kernel(
    ranks, b_hbm, a_hbm, p_hbm, out,
    stage, b_stage, a_high, a_low, b_high, b_low, y_high, y_low, c_high, c_low,
    work_a, into_a, near_a, slots_a,
    work_b, into_b, near_b, slots_b,
    work_g, into_g, slots_g, work_h, into_h, slots_h, marks,
    panel_one, panel_two, whole_one, whole_two, rings_one, rings_two,
    probe, gram, turn_one, turn_two,
    send, recv, local,
):
    clients, features, rank = b_hbm.shape
    p = probe.shape[1]
    slots = clients * rank
    cohort, feat = lax.axis_index("cohort"), lax.axis_index("feat")
    z, y = lax.div(cohort, NY), lax.rem(cohort, NY)
    x, core = lax.div(feat, 2), lax.rem(feat, 2)
    place = {
        "x": x, "y": y, "z": z, "core": core,
        "partner": (cohort, x * 2 + 1 - core),
        "feat": feat,
        "along_feat": lambda d: (cohort, lax.rem(feat + d, 2 * NX)),
        "along_x": lambda d: (cohort, lax.rem(x + d + NX, NX) * 2 + core),
        "along_y": lambda d: (z * NY + lax.rem(y + d + NY, NY), feat),
        "along_z": lambda d: (lax.rem(z + d + NZ, NZ) * NY + y, feat),
    }
    peers = []
    for axis, n in (("along_feat", 2 * NX), ("along_y", NY), ("along_z", NZ)):
        peers += [place[axis](d) for d in range(1, n)]

    barrier = pltpu.get_barrier_semaphore()
    for peer in peers:
        pl.semaphore_signal(barrier, inc=1, device_id=peer, device_id_type=MESH)

    def load(source, into, c, sem):
        start = pl.multiple_of(c * rank, rank)
        across = into is b_stage
        target = into.at[:, pl.ds(start, rank)] if across else into.at[pl.ds(start, rank), :]
        return pltpu.make_async_copy(source.at[c], target, local.at[sem])

    core, pairs = place["core"], clients // 2
    wanted = [2 * k + 1 - core for k in range(pairs)] + [2 * k + core for k in range(pairs)]
    load_p = pltpu.make_async_copy(p_hbm, probe, local.at[0])
    load_p.start()
    load_a = [load(a_hbm, stage, c, 1 + k) for k, c in enumerate(wanted)]
    load_b = [load(b_hbm, b_stage, c, 1 + clients + c) for c in range(clients)]
    for copy in load_a:
        copy.start()

    link = Link(send, recv)
    load_p.wait()
    y_high[...], y_low[...] = halves(probe[...])

    def client_coef(work, c, start, extent, begin, end):
        at, part = pl.ds(pl.multiple_of(c * rank, rank), rank), pl.ds(start, extent)
        total = product((a_high[at, part], a_low[at, part]), (y_high[part, :], y_low[part, :]))
        if not begin:
            total = total + work[at, :]
        if end:
            live = lax.broadcasted_iota(jnp.int32, total.shape, 0) < ranks[c]
            total = jnp.where(live, total, 0.0)
        work[at, :] = total

    def feat_stream(spaces, k, extent):
        work, into, near, slot_rows = spaces
        return feat_total(
            link, place, rows(work, k * extent, extent), rows(into, k * extent, extent),
            rows(near, k * extent // 2, extent // 2), rows(slot_rows, k * extent // 2, extent // 2),
            extent,
        )

    def coef_total(spaces, coef, *others):
        streams = [feat_stream(spaces, k, 2 * rank) for k in range(pairs)]
        for k, c in enumerate(wanted):
            coef(k, c)
            if k < pairs:
                next(streams[k])
        run(*streams, *others)

    def first_coef(k, c):
        load_a[k].wait()
        at = pl.ds(pl.multiple_of(c * rank, rank), rank)
        a_high[at, :], a_low[at, :] = halves(stage[at, :])
        if k == pairs - 1:
            for copy in load_b:
                copy.start()
        client_coef(work_a, c, 0, features, True, True)
        if k == 0:
            pl.semaphore_wait(barrier, len(peers))

    def b_stream():
        for c in range(clients):
            load_b[c].wait()
            across = pl.ds(c * rank, rank)
            for k in range(2):
                at = pl.ds(k * (features // 2), features // 2)
                b_high[at, across], b_low[at, across] = halves(b_stage[at, across])
            yield

    part = features // 4

    def panel_total(work, into, rings, done, *others):
        streams, open_streams = [], set(range(4))
        for k, kind in enumerate((lower_total, lower_total, upper_total, upper_total)):
            at = pl.ds(k * part, part)
            work[at, :] = product((b_high[at, :], b_low[at, :]), (c_high[...], c_low[...]))
            streams.append(
                kind(link, place, work, into, rows(rings, 2 * k * part, 2 * part), k * part, part)
            )
            next(streams[k])
        for kind in (0, 1, 0, 1, 0, 0, 1, 0, 1, 0):
            for k in (2 * kind, 2 * kind + 1):
                for other in others:
                    next(other, None)
                if k in open_streams and next(streams[k], part) == part:
                    open_streams.remove(k)
                    done(k, len(open_streams))
        run(*others)

    spaces_a = (work_a, into_a, near_a, slots_a)
    spaces_b = (work_b, into_b, near_b, slots_b)
    contract_rows = (((0,), (0,)), ((), ()))

    def split_rows(whole, k):
        at = pl.ds(k * part, part)
        y_high[at, :], y_low[at, :] = halves(whole[at, :])
        return at

    def add_gram(work, at, begin):
        value = (y_high[at, :], y_low[at, :])
        total = product(value, value, contract_rows)
        work[...] = total if begin else work[...] + total

    def gram_total(work, into, slot_rows):
        each = p // (2 * NX)
        ring = (place["feat"], 2 * NX, each, place["along_feat"])
        yield from reduce_direct(link, work, into, 0, *ring, slot_rows)
        yield from gather_direct(link, into, 0, *ring)

    def trace_total():
        square = whole_one[...] * whole_one[...]
        own = pl.ds(pl.multiple_of(place["feat"] * 8, 8), 8)
        marks[own, :] = jnp.sum(square.reshape(features // 8, 8, p), axis=0)
        yield from gather_direct(link, marks, 0, place["feat"], 2 * NX, 8, place["along_feat"])

    coef_total(spaces_a, first_coef, b_stream())
    c_high[...], c_low[...] = halves(into_a[...])

    last_part = []

    def first_done(k, left):
        at = split_rows(whole_one, k)
        if left:
            for c in range(clients):
                client_coef(work_b, c, k * part, part, left == 3, False)
        else:
            last_part.append(k * part)

    panel_total(panel_one, whole_one, rings_one, first_done)
    link.drain()

    coef_total(
        spaces_b, lambda k, c: client_coef(work_b, c, last_part[0], part, False, True), trace_total()
    )
    scale_one = inverse_root(jnp.sum(marks[...], keepdims=True))
    c_high[...], c_low[...] = halves(into_b[...] * scale_one)

    def first_turn():
        for k in range(4):
            add_gram(work_g, pl.ds(k * part, part), k == 0)
        yield from gram_total(work_g, into_g, slots_g)
        gram[...] = into_g[...] * (scale_one * scale_one)

    def second_done(k, left):
        add_gram(work_h, split_rows(whole_two, k), left == 3)

    panel_total(panel_two, whole_two, rings_two, second_done, first_turn())

    def first_applied():
        yield from newton(gram, turn_one)
        turn = halves(turn_one[...])
        for k in range(4):
            at = pl.ds(k * part, part)
            y_high[at, :], y_low[at, :] = halves(product((y_high[at, :], y_low[at, :]), turn))

    last_gram, applied = gram_total(work_h, into_h, slots_h), first_applied()
    next(last_gram)
    for turn in range(7):
        next(applied)
    next(last_gram)
    run(applied)
    run(last_gram)
    gram[...] = times(times(turn_one[...], into_h[...]), turn_one[...])
    scale = root_of_trace(gram[...])
    gram[...] = gram[...] * (scale * scale)
    run(newton(gram, turn_two))
    out[...] = product((y_high[...], y_low[...]), halves(turn_two[...] * (scale * math.sqrt(D))))
    link.drain()


def on_device(b_factors, a_factors, ranks, probes):
    clients, features, rank = b_factors.shape
    p = probes.shape[1]
    slots = clients * rank
    vm = pltpu.VMEM

    def feat_space(extent):
        return [
            vm((extent, p), F32), vm((extent, p), F32), vm((extent // 2, p), F32),
            vm((extent // 2, p), F32),
        ]

    scratch = (
        [vm((slots, features), F32), vm((features, slots), F32)]
        + [vm((slots, features), BF)] * 2
        + [vm((features, slots), BF)] * 2
        + [vm((features, p), BF)] * 2
        + [vm((slots, p), BF)] * 2
        + feat_space(slots) * 2 + [vm((p, p), F32)] * 6 + [vm((16 * NX, p), F32)]
        + [vm((features, p), F32)] * 4
        + [vm((2 * features, p), F32)] * 2
        + [vm((features, p), F32)]
        + [vm((p, p), F32)] * 3
        + [pltpu.SemaphoreType.DMA((280,)), pltpu.SemaphoreType.DMA((280,)), pltpu.SemaphoreType.DMA((1 + 2 * clients,))]
    )
    anywhere = pl.BlockSpec(memory_space=pltpu.MemorySpace.HBM)
    return pl.pallas_call(
        kernel,
        out_shape=jax.ShapeDtypeStruct((features, p), F32),
        in_specs=[pl.BlockSpec(memory_space=pltpu.SMEM), anywhere, anywhere, anywhere],
        out_specs=pl.BlockSpec(memory_space=pltpu.VMEM),
        scratch_shapes=scratch,
        compiler_params=pltpu.CompilerParams(
            collective_id=0, has_side_effects=True, vmem_limit_bytes=52 << 20
        ),
    )(ranks, b_factors, a_factors, probes)


def solution(mesh):
    in_specs = (P("cohort", "feat", None), P("cohort", None, "feat"), P("cohort"), P("feat", None))
    out_specs = P("feat", None)
    return jax.shard_map(
        on_device, mesh=mesh, in_specs=in_specs, out_specs=out_specs, check_vma=False
    )
```

```python
import functools
import math

import jax
import jax.numpy as jnp
from jax import lax
from jax.experimental import pallas as pl
from jax.experimental.pallas import tpu as pltpu
from jax.sharding import PartitionSpec as P

D = 8192
NS_STEPS = 5
NX, NY, NZ = 4, 4, 8
MESH = pl.DeviceIdType.MESH
FAR_FIRST = {4: (2, 1, 3), 8: (4, 3, 5, 2, 6, 1, 7)}
BF = jnp.bfloat16
F32 = jnp.float32


def rows(ref, start, size):
    if not isinstance(start, int):
        start = pl.multiple_of(start, 8)
    return ref.at[pl.ds(start, size), :]


class Link:
    def __init__(self, send, recv):
        self.send, self.recv, self.count, self.sent = send, recv, 0, []

    def copy(self, src, dst, device):
        copy = pltpu.make_async_remote_copy(
            src_ref=src,
            dst_ref=dst,
            send_sem=self.send.at[self.count],
            recv_sem=self.recv.at[self.count],
            device_id=device,
            device_id_type=MESH,
        )
        copy.start()
        self.count += 1
        self.sent.append(copy)
        return copy

    def drain(self):
        for copy in self.sent:
            copy.wait_send()
        self.sent = []


def take(copies):
    for copy in copies:
        copy.wait_recv()


def reduce_direct(link, work, into, base, at, n, size, device, slots, ready=None):
    coming = []
    for offset in FAR_FIRST[n]:
        start = base + lax.rem(at + offset, n) * size
        if ready is not None:
            ready(offset)
        coming.append(
            link.copy(
                rows(work, start, size), rows(slots, (offset - 1) * size, size), device(offset)
            )
        )
    if ready is not None:
        ready(0)
    yield
    take(coming)
    total = rows(work, base + at * size, size)[...]
    for step in range(n - 1):
        total = total + rows(slots, step * size, size)[...]
    rows(into, base + at * size, size)[...] = total


def gather_direct(link, into, base, at, n, size, device, also=None):
    own = rows(into, base + at * size, size)
    coming = [(offset, link.copy(own, own, device(offset))) for offset in FAR_FIRST[n]]
    if also is not None:
        also(own)
    yield
    for offset, copy in reversed(coming):
        copy.wait_recv()
        if also is not None:
            also(rows(into, base + lax.rem(at + n - offset, n) * size, size))


def reduce_pair_steps(link, work, into, base, at, n, size, device, slots):
    half = size // 2

    def shard(offset, skip, extent):
        return rows(work, base + lax.rem(at + offset + n, n) * size + skip, extent)

    def slot(index, extent):
        return rows(slots, index * size, extent)

    signs = ((1, 0, 0), (-1, half, 4))
    coming, straight, joined = {}, [], []
    for sign, skip, first in signs:
        coming[sign] = [
            link.copy(shard(4, skip, half), slot(first, half), device(2 * sign)),
            link.copy(shard(3 * sign, 0, size), slot(first + 1, size), device(sign)),
        ]
    for sign, skip, first in signs:
        straight.append(link.copy(shard(sign, 0, size), slot(first + 2, size), device(sign)))
    yield
    for sign, skip, first in signs:
        take(coming[sign])
        target = shard(2 * sign, 0, size)
        target[...] = target[...] + slot(first + 1, size)[...]
        part = shard(2 * sign, skip, half)
        part[...] = part[...] + slot(first, half)[...]
        joined.append(link.copy(target, slot(first + 3, size), device(2 * sign)))
    yield
    take(straight)
    take(joined)
    total = shard(0, 0, size)[...]
    for index in (2, 3, 6, 7):
        total = total + slot(index, size)[...]
    rows(into, base + at * size, size)[...] = total


def gather_pair_steps(link, into, base, at, n, size, device):
    half = size // 2

    def shard(offset, skip=0, extent=size):
        return rows(into, base + lax.rem(at + offset + n, n) * size + skip, extent)

    signs = ((1, 0), (-1, half))
    far = {sign: link.copy(shard(0), shard(0), device(2 * sign)) for sign, skip in signs}
    near = [link.copy(shard(0), shard(0), device(sign)) for sign, skip in signs]
    yield
    last = []
    for sign, skip in signs:
        far[sign].wait_recv()
        passed = shard(-2 * sign, skip, half)
        last.append(link.copy(passed, passed, device(2 * sign)))
        passed = shard(-2 * sign)
        last.append(link.copy(passed, passed, device(sign)))
    yield
    take(near)
    take(last)


def feat_total(link, place, work, into, near, slots, extent):
    half = extent // 2
    quarter = half // NX
    x, mine, other = place["x"], place["core"] * half, (1 - place["core"]) * half
    pairs = {}
    for offset in FAR_FIRST[NX] + (0,):
        start = lax.rem(x + offset, NX) * quarter
        pairs[offset] = (
            start,
            link.copy(rows(work, other + start, quarter), rows(near, start, quarter), place["partner"]),
        )
    yield

    def ready(offset):
        start, copy = pairs[offset]
        copy.wait_recv()
        target = rows(work, mine + start, quarter)
        target[...] = target[...] + rows(near, start, quarter)[...]

    yield from reduce_direct(
        link, work, into, mine, x, NX, quarter, place["along_x"], slots, ready
    )
    shared = []

    def also(ref):
        shared.append(link.copy(ref, ref, place["partner"]))

    yield from gather_direct(link, into, mine, x, NX, quarter, place["along_x"], also)
    yield
    take(shared)


def upper_total(link, place, work, into, slots, base, extent):
    y, z = place["y"], place["z"]
    size, small = extent // NY, extent // NY // NZ
    near = base + y * size
    along_y, along_z = place["along_y"], place["along_z"]
    yield from reduce_direct(link, work, work, base, y, NY, size, along_y, rows(slots, 0, extent))
    yield from reduce_direct(link, work, into, near, z, NZ, small, along_z, rows(slots, extent, size))
    yield from gather_direct(link, into, near, z, NZ, small, along_z)
    yield from gather_direct(link, into, base, y, NY, size, along_y)


def lower_total(link, place, work, into, slots, base, extent):
    y, z = place["y"], place["z"]
    size, small = extent // NZ, extent // NZ // NY
    near = base + z * size
    along_y, along_z = place["along_y"], place["along_z"]
    yield from reduce_pair_steps(link, work, work, base, z, NZ, size, along_z, rows(slots, 0, extent))
    yield from reduce_direct(link, work, into, near, y, NY, small, along_y, rows(slots, extent, size))
    yield from gather_direct(link, into, near, y, NY, small, along_y)
    yield from gather_pair_steps(link, into, base, z, NZ, size, along_z)


def run(*streams):
    streams = list(streams)
    while streams:
        for stream in list(streams):
            try:
                next(stream)
            except StopIteration:
                streams.remove(stream)


def halves(value):
    high = value.astype(BF)
    return high, (value - high.astype(F32)).astype(BF)


def dot(left, right, dims=(((1,), (0,)), ((), ()))):
    return lax.dot_general(left, right, dims, preferred_element_type=F32)


def product(left, right, dims=(((1,), (0,)), ((), ()))):
    (lh, ll), (rh, rl) = left, right
    return dot(lh, rh, dims) + (dot(lh, rl, dims) + dot(ll, rh, dims))


def times(left, right):
    return product(halves(left), halves(right))


def inverse_root(total):
    guess = lax.rsqrt(total)
    return guess * (1.5 - 0.5 * total * guess * guess)


def diagonal(p):
    return lax.broadcasted_iota(jnp.int32, (p, p), 0) == lax.broadcasted_iota(jnp.int32, (p, p), 1)


def root_of_trace(gram):
    total = jnp.sum(jnp.where(diagonal(gram.shape[0]), gram, 0.0), keepdims=True)
    return inverse_root(total)


def newton(gram, turn):
    for at in range(NS_STEPS):
        step = jnp.where(diagonal(gram.shape[0]), 1.5, 0.0) - 0.5 * gram[...]
        split = halves(step)
        turn[...] = step if at == 0 else product(halves(turn[...]), split)
        if at + 1 < NS_STEPS:
            for factor in range(2):
                yield
                gram[...] = product(halves(gram[...]), split)
            yield


def kernel(
    ranks, b_hbm, a_hbm, p_hbm, out,
    stage, b_stage, a_high, a_low, b_high, b_low, y_high, y_low, c_high, c_low,
    work_a, into_a, near_a, slots_a,
    work_b, into_b, near_b, slots_b,
    work_g, into_g, slots_g, work_h, into_h, slots_h, marks,
    panel_one, panel_two, whole_one, whole_two, rings_one, rings_two,
    probe, gram, turn_one, turn_two,
    send, recv, local,
):
    clients, features, rank = b_hbm.shape
    p = probe.shape[1]
    slots = clients * rank
    cohort, feat = lax.axis_index("cohort"), lax.axis_index("feat")
    z, y = lax.div(cohort, NY), lax.rem(cohort, NY)
    x, core = lax.div(feat, 2), lax.rem(feat, 2)
    place = {
        "x": x, "y": y, "z": z, "core": core,
        "partner": (cohort, x * 2 + 1 - core),
        "feat": feat,
        "along_feat": lambda d: (cohort, lax.rem(feat + d, 2 * NX)),
        "along_x": lambda d: (cohort, lax.rem(x + d + NX, NX) * 2 + core),
        "along_y": lambda d: (z * NY + lax.rem(y + d + NY, NY), feat),
        "along_z": lambda d: (lax.rem(z + d + NZ, NZ) * NY + y, feat),
    }
    peers = []
    for axis, n in (("along_feat", 2 * NX), ("along_y", NY), ("along_z", NZ)):
        peers += [place[axis](d) for d in range(1, n)]

    barrier = pltpu.get_barrier_semaphore()
    for peer in peers:
        pl.semaphore_signal(barrier, inc=1, device_id=peer, device_id_type=MESH)

    def load(source, into, c, sem):
        start = pl.multiple_of(c * rank, rank)
        across = into is b_stage
        target = into.at[:, pl.ds(start, rank)] if across else into.at[pl.ds(start, rank), :]
        return pltpu.make_async_copy(source.at[c], target, local.at[sem])

    core, pairs = place["core"], clients // 2
    wanted = [2 * k + 1 - core for k in range(pairs)] + [2 * k + core for k in range(pairs)]
    load_p = pltpu.make_async_copy(p_hbm, probe, local.at[0])
    load_p.start()
    load_a = [load(a_hbm, stage, c, 1 + k) for k, c in enumerate(wanted)]
    load_b = [load(b_hbm, b_stage, c, 1 + clients + c) for c in range(clients)]
    for copy in load_a:
        copy.start()

    link = Link(send, recv)
    load_p.wait()
    y_high[...], y_low[...] = halves(probe[...])

    def client_coef(work, c, start, extent, begin, end):
        at, part = pl.ds(pl.multiple_of(c * rank, rank), rank), pl.ds(start, extent)
        total = product((a_high[at, part], a_low[at, part]), (y_high[part, :], y_low[part, :]))
        if not begin:
            total = total + work[at, :]
        if end:
            live = lax.broadcasted_iota(jnp.int32, total.shape, 0) < ranks[c]
            total = jnp.where(live, total, 0.0)
        work[at, :] = total

    def feat_stream(spaces, k, extent):
        work, into, near, slot_rows = spaces
        return feat_total(
            link, place, rows(work, k * extent, extent), rows(into, k * extent, extent),
            rows(near, k * extent // 2, extent // 2), rows(slot_rows, k * extent // 2, extent // 2),
            extent,
        )

    def coef_total(spaces, coef, *others):
        streams = [feat_stream(spaces, k, 2 * rank) for k in range(pairs)]
        for k, c in enumerate(wanted):
            coef(k, c)
            if k < pairs:
                next(streams[k])
        run(*streams, *others)

    def first_coef(k, c):
        load_a[k].wait()
        at = pl.ds(pl.multiple_of(c * rank, rank), rank)
        a_high[at, :], a_low[at, :] = halves(stage[at, :])
        if k == pairs - 1:
            for copy in load_b:
                copy.start()
        client_coef(work_a, c, 0, features, True, True)
        if k == 0:
            pl.semaphore_wait(barrier, len(peers))

    def b_stream():
        for c in range(clients):
            load_b[c].wait()
            across = pl.ds(c * rank, rank)
            for k in range(2):
                at = pl.ds(k * (features // 2), features // 2)
                b_high[at, across], b_low[at, across] = halves(b_stage[at, across])
            yield

    part = features // 4

    def panel_total(work, into, rings, done, *others):
        streams, open_streams = [], set(range(4))
        for k, kind in enumerate((lower_total, lower_total, upper_total, upper_total)):
            at = pl.ds(k * part, part)
            work[at, :] = product((b_high[at, :], b_low[at, :]), (c_high[...], c_low[...]))
            streams.append(
                kind(link, place, work, into, rows(rings, 2 * k * part, 2 * part), k * part, part)
            )
            next(streams[k])
        for kind in (0, 1, 0, 1, 0, 0, 1, 0, 1, 0):
            for k in (2 * kind, 2 * kind + 1):
                for other in others:
                    next(other, None)
                if k in open_streams and next(streams[k], part) == part:
                    open_streams.remove(k)
                    done(k, len(open_streams))
        run(*others)

    spaces_a = (work_a, into_a, near_a, slots_a)
    spaces_b = (work_b, into_b, near_b, slots_b)
    contract_rows = (((0,), (0,)), ((), ()))

    def split_rows(whole, k):
        at = pl.ds(k * part, part)
        y_high[at, :], y_low[at, :] = halves(whole[at, :])
        return at

    def add_gram(work, at, begin):
        value = (y_high[at, :], y_low[at, :])
        total = product(value, value, contract_rows)
        work[...] = total if begin else work[...] + total

    def gram_total(work, into, slot_rows):
        each = p // (2 * NX)
        ring = (place["feat"], 2 * NX, each, place["along_feat"])
        yield from reduce_direct(link, work, into, 0, *ring, slot_rows)
        yield from gather_direct(link, into, 0, *ring)

    def trace_total():
        square = whole_one[...] * whole_one[...]
        own = pl.ds(pl.multiple_of(place["feat"] * 8, 8), 8)
        marks[own, :] = jnp.sum(square.reshape(features // 8, 8, p), axis=0)
        yield from gather_direct(link, marks, 0, place["feat"], 2 * NX, 8, place["along_feat"])

    coef_total(spaces_a, first_coef, b_stream())
    c_high[...], c_low[...] = halves(into_a[...])

    last_part = []

    def first_done(k, left):
        at = split_rows(whole_one, k)
        if left:
            for c in range(clients):
                client_coef(work_b, c, k * part, part, left == 3, False)
        else:
            last_part.append(k * part)

    panel_total(panel_one, whole_one, rings_one, first_done)
    link.drain()

    coef_total(
        spaces_b, lambda k, c: client_coef(work_b, c, last_part[0], part, False, True), trace_total()
    )
    scale_one = inverse_root(jnp.sum(marks[...], keepdims=True))
    c_high[...], c_low[...] = halves(into_b[...] * scale_one)

    def first_turn():
        for k in range(4):
            add_gram(work_g, pl.ds(k * part, part), k == 0)
        for leg in gram_total(work_g, into_g, slots_g):
            for rest in range(4):
                yield
        gram[...] = into_g[...] * (scale_one * scale_one)
        yield from newton(gram, turn_one)

    def second_done(k, left):
        add_gram(work_h, split_rows(whole_two, k), left == 3)

    panel_total(panel_two, whole_two, rings_two, second_done, first_turn())

    last_gram = gram_total(work_h, into_h, slots_h)
    next(last_gram)
    turn = halves(turn_one[...])
    for k in range(4):
        at = pl.ds(k * part, part)
        y_high[at, :], y_low[at, :] = halves(product((y_high[at, :], y_low[at, :]), turn))
    run(last_gram)
    gram[...] = times(times(turn_one[...], into_h[...]), turn_one[...])
    scale = root_of_trace(gram[...])
    gram[...] = gram[...] * (scale * scale)
    run(newton(gram, turn_two))
    out[...] = product((y_high[...], y_low[...]), halves(turn_two[...] * (scale * math.sqrt(D))))
    link.drain()


def on_device(b_factors, a_factors, ranks, probes):
    clients, features, rank = b_factors.shape
    p = probes.shape[1]
    slots = clients * rank
    vm = pltpu.VMEM

    def feat_space(extent):
        return [
            vm((extent, p), F32), vm((extent, p), F32), vm((extent // 2, p), F32),
            vm((extent // 2, p), F32),
        ]

    scratch = (
        [vm((slots, features), F32), vm((features, slots), F32)]
        + [vm((slots, features), BF)] * 2
        + [vm((features, slots), BF)] * 2
        + [vm((features, p), BF)] * 2
        + [vm((slots, p), BF)] * 2
        + feat_space(slots) * 2 + [vm((p, p), F32)] * 6 + [vm((16 * NX, p), F32)]
        + [vm((features, p), F32)] * 4
        + [vm((2 * features, p), F32)] * 2
        + [vm((features, p), F32)]
        + [vm((p, p), F32)] * 3
        + [pltpu.SemaphoreType.DMA((280,)), pltpu.SemaphoreType.DMA((280,)), pltpu.SemaphoreType.DMA((1 + 2 * clients,))]
    )
    anywhere = pl.BlockSpec(memory_space=pltpu.MemorySpace.HBM)
    return pl.pallas_call(
        kernel,
        out_shape=jax.ShapeDtypeStruct((features, p), F32),
        in_specs=[pl.BlockSpec(memory_space=pltpu.SMEM), anywhere, anywhere, anywhere],
        out_specs=pl.BlockSpec(memory_space=pltpu.VMEM),
        scratch_shapes=scratch,
        compiler_params=pltpu.CompilerParams(
            collective_id=0, has_side_effects=True, vmem_limit_bytes=52 << 20
        ),
    )(ranks, b_factors, a_factors, probes)


def solution(mesh):
    in_specs = (P("cohort", "feat", None), P("cohort", None, "feat"), P("cohort"), P("feat", None))
    out_specs = P("feat", None)
    return jax.shard_map(
        on_device, mesh=mesh, in_specs=in_specs, out_specs=out_specs, check_vma=False
    )
```

```python
import functools
import math

import jax
import jax.numpy as jnp
from jax import lax
from jax.experimental import pallas as pl
from jax.experimental.pallas import tpu as pltpu
from jax.sharding import PartitionSpec as P

D = 8192
NS_STEPS = 5
NX, NY, NZ = 4, 4, 8
MESH = pl.DeviceIdType.MESH
FAR_FIRST = {4: (2, 1, 3), 8: (4, 3, 5, 2, 6, 1, 7)}
BF = jnp.bfloat16
F32 = jnp.float32


def rows(ref, start, size):
    if not isinstance(start, int):
        start = pl.multiple_of(start, 8)
    return ref.at[pl.ds(start, size), :]


class Link:
    def __init__(self, send, recv):
        self.send, self.recv, self.count, self.sent = send, recv, 0, []

    def copy(self, src, dst, device):
        copy = pltpu.make_async_remote_copy(
            src_ref=src,
            dst_ref=dst,
            send_sem=self.send.at[self.count],
            recv_sem=self.recv.at[self.count],
            device_id=device,
            device_id_type=MESH,
        )
        copy.start()
        self.count += 1
        self.sent.append(copy)
        return copy

    def drain(self):
        for copy in self.sent:
            copy.wait_send()
        self.sent = []


def take(copies):
    for copy in copies:
        copy.wait_recv()


def reduce_direct(link, work, into, base, at, n, size, device, slots, ready=None):
    coming = []
    for offset in FAR_FIRST[n]:
        start = base + lax.rem(at + offset, n) * size
        if ready is not None:
            ready(offset)
        coming.append(
            link.copy(
                rows(work, start, size), rows(slots, (offset - 1) * size, size), device(offset)
            )
        )
    if ready is not None:
        ready(0)
    yield
    take(coming)
    total = rows(work, base + at * size, size)[...]
    for step in range(n - 1):
        total = total + rows(slots, step * size, size)[...]
    rows(into, base + at * size, size)[...] = total


def gather_direct(link, into, base, at, n, size, device, also=None):
    own = rows(into, base + at * size, size)
    coming = [(offset, link.copy(own, own, device(offset))) for offset in FAR_FIRST[n]]
    if also is not None:
        also(own)
    yield
    for offset, copy in reversed(coming):
        copy.wait_recv()
        if also is not None:
            also(rows(into, base + lax.rem(at + n - offset, n) * size, size))


def reduce_pair_steps(link, work, into, base, at, n, size, device, slots):
    half = size // 2

    def shard(offset, skip, extent):
        return rows(work, base + lax.rem(at + offset + n, n) * size + skip, extent)

    def slot(index, extent):
        return rows(slots, index * size, extent)

    signs = ((1, 0, 0), (-1, half, 4))
    coming, straight, joined = {}, [], []
    for sign, skip, first in signs:
        coming[sign] = [
            link.copy(shard(4, skip, half), slot(first, half), device(2 * sign)),
            link.copy(shard(3 * sign, 0, size), slot(first + 1, size), device(sign)),
        ]
    for sign, skip, first in signs:
        straight.append(link.copy(shard(sign, 0, size), slot(first + 2, size), device(sign)))
    yield
    for sign, skip, first in signs:
        take(coming[sign])
        target = shard(2 * sign, 0, size)
        target[...] = target[...] + slot(first + 1, size)[...]
        part = shard(2 * sign, skip, half)
        part[...] = part[...] + slot(first, half)[...]
        joined.append(link.copy(target, slot(first + 3, size), device(2 * sign)))
    yield
    take(straight)
    take(joined)
    total = shard(0, 0, size)[...]
    for index in (2, 3, 6, 7):
        total = total + slot(index, size)[...]
    rows(into, base + at * size, size)[...] = total


def gather_pair_steps(link, into, base, at, n, size, device):
    half = size // 2

    def shard(offset, skip=0, extent=size):
        return rows(into, base + lax.rem(at + offset + n, n) * size + skip, extent)

    signs = ((1, 0), (-1, half))
    far = {sign: link.copy(shard(0), shard(0), device(2 * sign)) for sign, skip in signs}
    near = [link.copy(shard(0), shard(0), device(sign)) for sign, skip in signs]
    yield
    last = []
    for sign, skip in signs:
        far[sign].wait_recv()
        passed = shard(-2 * sign, skip, half)
        last.append(link.copy(passed, passed, device(2 * sign)))
        passed = shard(-2 * sign)
        last.append(link.copy(passed, passed, device(sign)))
    yield
    take(near)
    take(last)


def feat_total(link, place, work, into, near, slots, extent):
    half = extent // 2
    quarter = half // NX
    x, mine, other = place["x"], place["core"] * half, (1 - place["core"]) * half
    pairs = {}
    for offset in FAR_FIRST[NX] + (0,):
        start = lax.rem(x + offset, NX) * quarter
        pairs[offset] = (
            start,
            link.copy(rows(work, other + start, quarter), rows(near, start, quarter), place["partner"]),
        )
    yield

    def ready(offset):
        start, copy = pairs[offset]
        copy.wait_recv()
        target = rows(work, mine + start, quarter)
        target[...] = target[...] + rows(near, start, quarter)[...]

    yield from reduce_direct(
        link, work, into, mine, x, NX, quarter, place["along_x"], slots, ready
    )
    shared = []

    def also(ref):
        shared.append(link.copy(ref, ref, place["partner"]))

    yield from gather_direct(link, into, mine, x, NX, quarter, place["along_x"], also)
    yield
    take(shared)


def upper_total(link, place, work, into, slots, base, extent):
    y, z = place["y"], place["z"]
    size, small = extent // NY, extent // NY // NZ
    near = base + y * size
    along_y, along_z = place["along_y"], place["along_z"]
    yield from reduce_direct(link, work, work, base, y, NY, size, along_y, rows(slots, 0, extent))
    yield from reduce_direct(link, work, into, near, z, NZ, small, along_z, rows(slots, extent, size))
    yield from gather_direct(link, into, near, z, NZ, small, along_z)
    yield from gather_direct(link, into, base, y, NY, size, along_y)


def lower_total(link, place, work, into, slots, base, extent):
    y, z = place["y"], place["z"]
    size, small = extent // NZ, extent // NZ // NY
    near = base + z * size
    along_y, along_z = place["along_y"], place["along_z"]
    yield from reduce_pair_steps(link, work, work, base, z, NZ, size, along_z, rows(slots, 0, extent))
    yield from reduce_direct(link, work, into, near, y, NY, small, along_y, rows(slots, extent, size))
    yield from gather_direct(link, into, near, y, NY, small, along_y)
    yield from gather_pair_steps(link, into, base, z, NZ, size, along_z)


def run(*streams):
    streams = list(streams)
    while streams:
        for stream in list(streams):
            try:
                next(stream)
            except StopIteration:
                streams.remove(stream)


def halves(value):
    high = value.astype(BF)
    return high, (value - high.astype(F32)).astype(BF)


def dot(left, right, dims=(((1,), (0,)), ((), ()))):
    return lax.dot_general(left, right, dims, preferred_element_type=F32)


def product(left, right, dims=(((1,), (0,)), ((), ()))):
    (lh, ll), (rh, rl) = left, right
    return dot(lh, rh, dims) + (dot(lh, rl, dims) + dot(ll, rh, dims))


def times(left, right):
    return product(halves(left), halves(right))


def inverse_root(total):
    guess = lax.rsqrt(total)
    return guess * (1.5 - 0.5 * total * guess * guess)


def diagonal(p):
    return lax.broadcasted_iota(jnp.int32, (p, p), 0) == lax.broadcasted_iota(jnp.int32, (p, p), 1)


def root_of_trace(gram):
    total = jnp.sum(jnp.where(diagonal(gram.shape[0]), gram, 0.0), keepdims=True)
    return inverse_root(total)


def newton(gram, turn):
    for at in range(NS_STEPS):
        step = jnp.where(diagonal(gram.shape[0]), 1.5, 0.0) - 0.5 * gram[...]
        split = halves(step)
        turn[...] = step if at == 0 else product(halves(turn[...]), split)
        if at + 1 < NS_STEPS:
            for factor in range(2):
                yield
                gram[...] = product(halves(gram[...]), split)
            yield


def kernel(
    ranks, b_hbm, a_hbm, p_hbm, out,
    stage, b_stage, a_high, a_low, b_high, b_low, y_high, y_low, c_high, c_low,
    work_a, into_a, near_a, slots_a,
    work_b, into_b, near_b, slots_b,
    work_g, into_g, slots_g, work_h, into_h, slots_h, marks,
    panel_one, panel_two, whole_one, whole_two, rings_one, rings_two,
    probe, gram, turn_one, turn_two,
    send, recv, local,
):
    clients, features, rank = b_hbm.shape
    p = probe.shape[1]
    slots = clients * rank
    cohort, feat = lax.axis_index("cohort"), lax.axis_index("feat")
    z, y = lax.div(cohort, NY), lax.rem(cohort, NY)
    x, core = lax.div(feat, 2), lax.rem(feat, 2)
    place = {
        "x": x, "y": y, "z": z, "core": core,
        "partner": (cohort, x * 2 + 1 - core),
        "feat": feat,
        "along_feat": lambda d: (cohort, lax.rem(feat + d, 2 * NX)),
        "along_x": lambda d: (cohort, lax.rem(x + d + NX, NX) * 2 + core),
        "along_y": lambda d: (z * NY + lax.rem(y + d + NY, NY), feat),
        "along_z": lambda d: (lax.rem(z + d + NZ, NZ) * NY + y, feat),
    }
    peers = []
    for axis, n in (("along_feat", 2 * NX), ("along_y", NY), ("along_z", NZ)):
        peers += [place[axis](d) for d in range(1, n)]

    barrier = pltpu.get_barrier_semaphore()
    for peer in peers:
        pl.semaphore_signal(barrier, inc=1, device_id=peer, device_id_type=MESH)

    def load(source, into, c, sem):
        start = pl.multiple_of(c * rank, rank)
        across = into is b_stage
        target = into.at[:, pl.ds(start, rank)] if across else into.at[pl.ds(start, rank), :]
        return pltpu.make_async_copy(source.at[c], target, local.at[sem])

    core, pairs = place["core"], clients // 2
    wanted = [2 * k + 1 - core for k in range(pairs)] + [2 * k + core for k in range(pairs)]
    load_p = pltpu.make_async_copy(p_hbm, probe, local.at[0])
    load_p.start()
    load_a = [load(a_hbm, stage, c, 1 + k) for k, c in enumerate(wanted)]
    load_b = [load(b_hbm, b_stage, c, 1 + clients + c) for c in range(clients)]
    for copy in load_a:
        copy.start()

    link = Link(send, recv)
    load_p.wait()
    y_high[...], y_low[...] = halves(probe[...])

    def client_coef(work, c, start, extent, begin, end):
        at, part = pl.ds(pl.multiple_of(c * rank, rank), rank), pl.ds(start, extent)
        total = product((a_high[at, part], a_low[at, part]), (y_high[part, :], y_low[part, :]))
        if not begin:
            total = total + work[at, :]
        if end:
            live = lax.broadcasted_iota(jnp.int32, total.shape, 0) < ranks[c]
            total = jnp.where(live, total, 0.0)
        work[at, :] = total

    def feat_stream(spaces, k, extent):
        work, into, near, slot_rows = spaces
        return feat_total(
            link, place, rows(work, k * extent, extent), rows(into, k * extent, extent),
            rows(near, k * extent // 2, extent // 2), rows(slot_rows, k * extent // 2, extent // 2),
            extent,
        )

    def coef_total(spaces, coef, early, *others):
        streams = [feat_stream(spaces, k, 2 * rank) for k in range(pairs)]
        for k, c in enumerate(wanted):
            coef(k, c)
            if k < pairs:
                next(streams[k])
        for turn in range(3):
            for stream in (*streams, *others):
                next(stream, None)
        run(*others)
        early()
        run(*streams)

    def first_coef(k, c):
        load_a[k].wait()
        at = pl.ds(pl.multiple_of(c * rank, rank), rank)
        a_high[at, :], a_low[at, :] = halves(stage[at, :])
        if k == pairs - 1:
            for copy in load_b:
                copy.start()
        client_coef(work_a, c, 0, features, True, True)
        if k == 0:
            pl.semaphore_wait(barrier, len(peers))

    def b_stream():
        for c in range(clients):
            load_b[c].wait()
            across = pl.ds(c * rank, rank)
            for k in range(2):
                at = pl.ds(k * (features // 2), features // 2)
                b_high[at, across], b_low[at, across] = halves(b_stage[at, across])
            yield

    part = features // 4

    def split_coef(coef, chosen, scale=None):
        for c in chosen:
            at = pl.ds(pl.multiple_of(c * rank, rank), rank)
            value = coef[at, :] if scale is None else coef[at, :] * scale
            c_high[at, :], c_low[at, :] = halves(value)

    def panel_part(work, at, chosen, begin):
        total = None if begin else work[at, :]
        for c in chosen:
            over = pl.ds(pl.multiple_of(c * rank, rank), rank)
            term = product((b_high[at, over], b_low[at, over]), (c_high[over, :], c_low[over, :]))
            total = term if total is None else total + term
        work[at, :] = total

    def panel_begin(work):
        for k in range(4):
            panel_part(work, pl.ds(k * part, part), wanted[pairs:], True)

    def panel_total(work, into, rings, done, *others):
        streams, open_streams = [], set(range(4))
        for k, kind in enumerate((lower_total, lower_total, upper_total, upper_total)):
            at = pl.ds(k * part, part)
            panel_part(work, at, wanted[:pairs], False)
            streams.append(
                kind(link, place, work, into, rows(rings, 2 * k * part, 2 * part), k * part, part)
            )
            next(streams[k])
        for kind in (0, 1, 0, 1, 0, 0, 1, 0, 1, 0):
            for k in (2 * kind, 2 * kind + 1):
                for other in others:
                    next(other, None)
                if k in open_streams and next(streams[k], part) == part:
                    open_streams.remove(k)
                    done(k, len(open_streams))
        run(*others)

    spaces_a = (work_a, into_a, near_a, slots_a)
    spaces_b = (work_b, into_b, near_b, slots_b)
    contract_rows = (((0,), (0,)), ((), ()))

    def split_rows(whole, k):
        at = pl.ds(k * part, part)
        y_high[at, :], y_low[at, :] = halves(whole[at, :])
        return at

    def add_gram(work, at, begin):
        value = (y_high[at, :], y_low[at, :])
        total = product(value, value, contract_rows)
        work[...] = total if begin else work[...] + total

    def gram_total(work, into, slot_rows):
        each = p // (2 * NX)
        ring = (place["feat"], 2 * NX, each, place["along_feat"])
        yield from reduce_direct(link, work, into, 0, *ring, slot_rows)
        yield from gather_direct(link, into, 0, *ring)

    def trace_total():
        square = whole_one[...] * whole_one[...]
        own = pl.ds(pl.multiple_of(place["feat"] * 8, 8), 8)
        marks[own, :] = jnp.sum(square.reshape(features // 8, 8, p), axis=0)
        yield from gather_direct(link, marks, 0, place["feat"], 2 * NX, 8, place["along_feat"])

    def first_early():
        split_coef(into_a, wanted[pairs:])
        panel_begin(panel_one)

    coef_total(spaces_a, first_coef, first_early, b_stream())
    split_coef(into_a, wanted[:pairs])

    last_part = []

    def first_done(k, left):
        at = split_rows(whole_one, k)
        if left:
            for c in range(clients):
                client_coef(work_b, c, k * part, part, left == 3, False)
        else:
            last_part.append(k * part)

    panel_total(panel_one, whole_one, rings_one, first_done)
    link.drain()

    def root_one():
        return inverse_root(jnp.sum(marks[...], keepdims=True))

    def second_early():
        split_coef(into_b, wanted[pairs:], root_one())
        panel_begin(panel_two)

    def second_coef(k, c):
        client_coef(work_b, c, last_part[0], part, False, True)

    coef_total(spaces_b, second_coef, second_early, trace_total())
    scale_one = root_one()
    split_coef(into_b, wanted[:pairs], scale_one)

    def first_turn():
        for k in range(4):
            add_gram(work_g, pl.ds(k * part, part), k == 0)
        for leg in gram_total(work_g, into_g, slots_g):
            for rest in range(4):
                yield
        gram[...] = into_g[...] * (scale_one * scale_one)
        yield from newton(gram, turn_one)

    def second_done(k, left):
        add_gram(work_h, split_rows(whole_two, k), left == 3)

    panel_total(panel_two, whole_two, rings_two, second_done, first_turn())

    last_gram = gram_total(work_h, into_h, slots_h)
    next(last_gram)
    turn = halves(turn_one[...])
    for k in range(4):
        at = pl.ds(k * part, part)
        y_high[at, :], y_low[at, :] = halves(product((y_high[at, :], y_low[at, :]), turn))
    run(last_gram)
    gram[...] = times(times(turn_one[...], into_h[...]), turn_one[...])
    scale = root_of_trace(gram[...])
    gram[...] = gram[...] * (scale * scale)
    run(newton(gram, turn_two))
    out[...] = product((y_high[...], y_low[...]), halves(turn_two[...] * (scale * math.sqrt(D))))
    link.drain()


def on_device(b_factors, a_factors, ranks, probes):
    clients, features, rank = b_factors.shape
    p = probes.shape[1]
    slots = clients * rank
    vm = pltpu.VMEM

    def feat_space(extent):
        return [
            vm((extent, p), F32), vm((extent, p), F32), vm((extent // 2, p), F32),
            vm((extent // 2, p), F32),
        ]

    scratch = (
        [vm((slots, features), F32), vm((features, slots), F32)]
        + [vm((slots, features), BF)] * 2
        + [vm((features, slots), BF)] * 2
        + [vm((features, p), BF)] * 2
        + [vm((slots, p), BF)] * 2
        + feat_space(slots) * 2 + [vm((p, p), F32)] * 6 + [vm((16 * NX, p), F32)]
        + [vm((features, p), F32)] * 4
        + [vm((2 * features, p), F32)] * 2
        + [vm((features, p), F32)]
        + [vm((p, p), F32)] * 3
        + [pltpu.SemaphoreType.DMA((280,)), pltpu.SemaphoreType.DMA((280,)), pltpu.SemaphoreType.DMA((1 + 2 * clients,))]
    )
    anywhere = pl.BlockSpec(memory_space=pltpu.MemorySpace.HBM)
    return pl.pallas_call(
        kernel,
        out_shape=jax.ShapeDtypeStruct((features, p), F32),
        in_specs=[pl.BlockSpec(memory_space=pltpu.SMEM), anywhere, anywhere, anywhere],
        out_specs=pl.BlockSpec(memory_space=pltpu.VMEM),
        scratch_shapes=scratch,
        compiler_params=pltpu.CompilerParams(
            collective_id=0, has_side_effects=True, vmem_limit_bytes=52 << 20
        ),
    )(ranks, b_factors, a_factors, probes)


def solution(mesh):
    in_specs = (P("cohort", "feat", None), P("cohort", None, "feat"), P("cohort"), P("feat", None))
    out_specs = P("feat", None)
    return jax.shard_map(
        on_device, mesh=mesh, in_specs=in_specs, out_specs=out_specs, check_vma=False
    )
```
